32 devices in a mesh: cuts: 2 (over y), gx: 4 (over z), gy: 2 (over x), ma: 2 (over core).
Axes of the slice: x: 2, y: 2, z: 4, core: 2. Of those that a mesh axis runs over, the one named last changes fastest.
Arguments:
- eigen_modes: bfloat16 [4, 32, 32, 2, 3, 512], P('cuts', 'gx', 'gy', None, None, 'ma'), parts along dimension 0, may hold values from -0.25 to 0.25
- links_first: bfloat16 [4, 3, 3, 32, 32, 2], P('cuts', None, None, 'gx', 'gy'), parts along dimension 0, may hold values from -2.5 to 2.5
- links_second: bfloat16 [4, 3, 3, 32, 32, 2], P('cuts', None, None, 'gx', 'gy'), parts along dimension 0, may hold values from -2.5 to 2.5
Outputs:
- elementals: float32 [4, 2, 512, 512], P('cuts', None, ('gx', 'gy'), 'ma'), parts along dimension 0
The draws below stay inside these ranges and needn't reach their ends.
There are 2 independent parts, one for each index of `cuts`. The reference program is written for one: setup_inputs(seed, part) draws one part's arguments, and reference() takes and returns one part's arrays. A program takes and returns all parts, laid end to end along the dimension named above; each array names one. Nothing has to cross between parts.
All inputs are finite; a program needn't handle non-finite values.
Results may differ from the reference program's by a relative error of at most 0.0055.
Values may be sent and summed in bfloat16 or wider, within the bound.
A program may use at most 64 MiB of HBM per device.

```python
import jax
import jax.numpy as jnp
from jax import lax

NEV = 512
NZ = 2
NX = 32
NY = 32


def spiked(drawn, stream_key, source, target, parts, factor):
    def block_of(position):
        return (jnp.arange(drawn.shape[position]) // (drawn.shape[position] // parts)).reshape((-1,) + (1,) * (drawn.ndim - 1 - position))

    near = jax.random.permutation(stream_key, parts)[block_of(target)]
    far = (block_of(target) + parts // 2) % parts
    return jnp.where((block_of(source) == near) | (block_of(source) == far), factor * drawn, drawn)


def block_levels(rng, extent, split, low, largest):
    factor_of, own = 1.0, jax.random.fold_in(rng, 6)
    for position, parts in split:
        heights = jnp.exp(jax.random.uniform(jax.random.fold_in(own, position), (parts,), jnp.float32, low / len(split), largest / len(split)))
        factor_of = factor_of * jnp.repeat(heights, extent[position] // parts).reshape([-1 if axis == position else 1 for axis in range(len(extent))])
    return factor_of


def scatter_about(stream_key, shape, scale, limit, cuts=(), dtype=jnp.bfloat16):
    values = scale * jax.random.normal(stream_key, shape, jnp.float32)
    if cuts:
        values = values * block_levels(stream_key, shape, cuts, -0.22, 0.18)
    return jnp.clip(values, -limit, limit).astype(dtype)


def gaussian_with(key, dims, scale, reach, split, heavy, dtype=jnp.bfloat16):
    drawn = scale * jax.random.normal(key, dims, jnp.float32)
    if split:
        drawn = drawn * block_levels(key, dims, split, -0.22, 0.18)
    return jnp.clip(spiked(drawn, jax.random.fold_in(key, 3), *heavy), -reach, reach).astype(dtype)


def setup_inputs(seed: int = 0, part: int = 0) -> dict:
    seeds = jax.random.split(jax.random.key(seed), 4)
    part_keys = jax.random.split(jax.random.fold_in(seeds[3], part), 4)
    eigen_modes = gaussian_with(part_keys[0], (2, NX, NY, NZ, 3, NEV), 0.03, 0.25, ((1, 4), (2, 2), (5, 2)), (1, 5, 4, 2.0))
    links_first = scatter_about(part_keys[1], (2, 3, 3, NX, NY, NZ), 0.41, 2.5, ((3, 4), (4, 2)))
    links_second = scatter_about(part_keys[2], (2, 3, 3, NX, NY, NZ), 0.41, 2.5, ((3, 4), (4, 2)))
    return {"eigen_modes": eigen_modes, "links_first": links_first, "links_second": links_second}


def split_links(linkage):
    real_part = jnp.transpose(linkage[0].astype(jnp.float32), (2, 3, 4, 0, 1))
    imag_part = jnp.transpose(linkage[1].astype(jnp.float32), (2, 3, 4, 0, 1))
    return real_part, imag_part


def apply_link(link_real, link_imag, field, dagger):
    if dagger:
        form = "xyzba,xyzbm->xyzam"
        factor = -1.0
    else:
        form = "xyzab,xyzbm->xyzam"
        factor = 1.0
    high = lax.Precision.HIGHEST
    real_out = jnp.einsum(form, link_real, field[0], precision=high) - factor * jnp.einsum(form, link_imag, field[1], precision=high)
    imag_out = jnp.einsum(form, link_real, field[1], precision=high) + factor * jnp.einsum(form, link_imag, field[0], precision=high)
    return jnp.stack([real_out, imag_out])


def covariant(link_real, link_imag, field, lattice_axis):
    forward = jnp.roll(field, -1, lattice_axis)
    backward = jnp.roll(apply_link(link_real, link_imag, field, True), 1, lattice_axis)
    return apply_link(link_real, link_imag, forward, False) - backward


def contract(left, right_side):
    return lax.dot_general(left, right_side, (((0,), (0,)), ((), ())), preferred_element_type=jnp.float32)


def reference(eigen_modes, links_first, links_second):
    first_real, first_imag = split_links(links_first)
    second_real, second_imag = split_links(links_second)
    block_width = 128
    nblocks = NEV // block_width
    vec_real = eigen_modes[0].reshape(-1, NEV)
    vec_imag = eigen_modes[1].reshape(-1, NEV)
    blocks = jnp.moveaxis(eigen_modes.reshape(2, NX, NY, NZ, 3, nblocks, block_width), 5, 0)

    def one_block(block_modes):
        field = block_modes.astype(jnp.float32)
        disp_x = covariant(first_real, first_imag, field, 1).astype(jnp.bfloat16)
        disp_xy = covariant(second_real, second_imag, disp_x.astype(jnp.float32), 2).astype(jnp.bfloat16)
        results = []
        for shifted in (disp_x, disp_xy):
            sh_real = shifted[0].reshape(-1, block_width)
            sh_imag = shifted[1].reshape(-1, block_width)
            real_out = contract(vec_real, sh_real) + contract(vec_imag, sh_imag)
            imag_out = contract(vec_real, sh_imag) - contract(vec_imag, sh_real)
            results.append(jnp.stack([real_out, imag_out]))
        return jnp.stack(results)

    stacked = lax.map(one_block, blocks)
    return jnp.moveaxis(stacked, 0, 3).reshape(2, 2, NEV, NEV)
```

```python
import functools

import jax
import jax.numpy as jnp
from jax import lax
from jax.experimental import pallas as pl
from jax.experimental.pallas import tpu as pltpu
from jax.sharding import PartitionSpec as P

MESH = pl.DeviceIdType.MESH


def shifted(block, axis, distance):
    devices = range(lax.axis_size(axis))
    route = [((i - distance) % len(devices), i) for i in devices]
    return lax.ppermute(block, axis, route)


def apply_link(linkage, field, dagger):
    link_real = linkage[0].astype(jnp.float32)
    link_imag = linkage[1].astype(jnp.float32)
    factor = -1.0 if dagger else 1.0
    real_rows = []
    imag_rows = []
    for row in range(3):
        real_acc = None
        imag_acc = None
        for col in range(3):
            if dagger:
                coef_real = link_real[col, row][..., None]
                coef_imag = link_imag[col, row][..., None]
            else:
                coef_real = link_real[row, col][..., None]
                coef_imag = link_imag[row, col][..., None]
            field_real = field[0, col]
            field_imag = field[1, col]
            term_real = coef_real * field_real - factor * coef_imag * field_imag
            term_imag = coef_real * field_imag + factor * coef_imag * field_real
            real_acc = term_real if real_acc is None else real_acc + term_real
            imag_acc = term_imag if imag_acc is None else imag_acc + term_imag
        real_rows.append(real_acc)
        imag_rows.append(imag_acc)
    return jnp.stack([jnp.stack(real_rows), jnp.stack(imag_rows)])


def contract(left, right_side):
    return lax.dot_general(
        left, right_side, (((0,), (0,)), ((), ())), preferred_element_type=jnp.float32
    )


def rs_kernel(nx, left_ref, rx_ref, ry_ref, out_ref, own, xsend, xrecv, zsend, zrecv,
              xs_sem, xr_sem, zs_sem, zr_sem):
    gx = lax.axis_index("gx")
    gy = lax.axis_index("gy")
    other = 1 - gy
    rows = out_ref.shape[2]

    barrier = pltpu.get_barrier_semaphore()
    pl.semaphore_signal(barrier, inc=1, device_id={"gy": other}, device_id_type=MESH)
    for off in range(1, nx):
        pl.semaphore_signal(
            barrier, inc=1, device_id={"gx": lax.rem(gx + off, nx)}, device_id_type=MESH
        )
    pl.semaphore_wait(barrier, nx)

    offsets = sorted(range(1, nx), key=lambda o: -min(o, nx - o)) + [0]
    rights = (rx_ref, ry_ref)
    depth = left_ref.shape[2]
    x_copies = []
    for k, off in enumerate(offsets):
        dest = lax.rem(gx + off, nx)
        base = pl.multiple_of(dest * (2 * rows), 2 * rows)
        left_real = left_ref[0, pl.ds(base, 2 * rows), :]
        left_imag = left_ref[1, pl.ds(base, 2 * rows), :]
        for d in range(2):
            c = 2 * k + d
            right_real = rights[d][0]
            right_imag = rights[d][1]
            dot = functools.partial(jnp.dot, preferred_element_type=jnp.float32)
            real = dot(left_real, right_real) + dot(left_imag, right_imag)
            imag = dot(left_real, right_imag) - dot(left_imag, right_real)
            first = jnp.stack([real[:rows], imag[:rows]])
            second = jnp.stack([real[rows:], imag[rows:]])
            own[c] = jnp.where(gy == 0, first, second)
            xsend[c] = jnp.where(gy == 0, second, first).astype(xsend.dtype)
            copy = pltpu.make_async_remote_copy(
                src_ref=xsend.at[c],
                dst_ref=xrecv.at[c],
                send_sem=xs_sem.at[c],
                recv_sem=xr_sem.at[c],
                device_id={"gy": other},
                device_id_type=MESH,
            )
            copy.start()
            x_copies.append(copy)
    z_copies = []
    for k, off in enumerate(offsets):
        for d in range(2):
            c = 2 * k + d
            x_copies[c].wait()
            total = own[c] + xrecv[c].astype(jnp.float32)
            if off == 0:
                own[c] = total
                continue
            zsend[c] = total.astype(zsend.dtype)
            copy = pltpu.make_async_remote_copy(
                src_ref=zsend.at[c],
                dst_ref=zrecv.at[c],
                send_sem=zs_sem.at[c],
                recv_sem=zr_sem.at[c],
                device_id={"gx": lax.rem(gx + off, nx)},
                device_id_type=MESH,
            )
            copy.start()
            z_copies.append(copy)
    last = 2 * (nx - 1)
    for d in range(2):
        total = own[last + d]
        for k in range(nx - 1):
            z_copies[2 * k + d].wait()
            total = total + zrecv[2 * k + d].astype(jnp.float32)
        out_ref[d] = total


def reduce_projections(left, right_x, right_y):
    nx = lax.axis_size("gx")
    rows = left.shape[1] // (nx * 2)
    width = right_x.shape[2]
    count = 2 * nx
    vmem = pl.BlockSpec(memory_space=pltpu.VMEM)
    return pl.pallas_call(
        functools.partial(rs_kernel, nx),
        out_shape=jax.ShapeDtypeStruct((2, 2, rows, width), jnp.float32),
        in_specs=[vmem] * 3,
        out_specs=vmem,
        scratch_shapes=[
            pltpu.VMEM((count, 2, rows, width), jnp.float32),
            pltpu.VMEM((count, 2, rows, width), jnp.bfloat16),
            pltpu.VMEM((count, 2, rows, width), jnp.bfloat16),
            pltpu.VMEM((count - 2, 2, rows, width), jnp.bfloat16),
            pltpu.VMEM((count - 2, 2, rows, width), jnp.bfloat16),
            pltpu.SemaphoreType.DMA((count,)),
            pltpu.SemaphoreType.DMA((count,)),
            pltpu.SemaphoreType.DMA((count - 2,)),
            pltpu.SemaphoreType.DMA((count - 2,)),
        ],
        compiler_params=pltpu.CompilerParams(collective_id=0, has_side_effects=True),
    )(left, right_x, right_y)


def local(eigen_modes, links_first, links_second):
    width = eigen_modes.shape[5]
    modes = jnp.transpose(eigen_modes, (0, 4, 1, 2, 3, 5))
    upper = shifted(modes[:, :, :1], "gx", -1)
    lower = shifted(modes[:, :, -1:], "gx", 1)
    lower_links = shifted(links_first[:, :, :, -1:], "gx", 1)
    lower_links_y = shifted(links_second[:, :, :, :, -1:], "gy", 1)
    field = modes.astype(jnp.float32)
    forward = jnp.concatenate([modes[:, :, 1:], upper], axis=2).astype(jnp.float32)
    linked = apply_link(links_first[:, :, :, :-1], field[:, :, :-1], True)
    behind = apply_link(lower_links, lower.astype(jnp.float32), True)
    backward = jnp.concatenate([behind, linked], axis=2)
    disp_x = (apply_link(links_first, forward, False) - backward).astype(jnp.bfloat16)
    upper_row = shifted(disp_x[:, :, :, :1], "gy", -1)
    lower_row = shifted(disp_x[:, :, :, -1:], "gy", 1)
    forward_y = jnp.concatenate([disp_x[:, :, :, 1:], upper_row], axis=3).astype(jnp.float32)
    linked_y = apply_link(links_second[:, :, :, :, :-1], disp_x[:, :, :, :-1].astype(jnp.float32), True)
    behind_y = apply_link(lower_links_y, lower_row.astype(jnp.float32), True)
    backward_y = jnp.concatenate([behind_y, linked_y], axis=3)
    disp_xy = (apply_link(links_second, forward_y, False) - backward_y).astype(jnp.bfloat16)
    right_x = disp_x.reshape(2, -1, width)
    right_y = disp_xy.reshape(2, -1, width)
    ng, ny, nm = lax.axis_size("gx"), lax.axis_size("gy"), lax.axis_size("ma")
    rows = width * nm // (ng * ny)
    if ny == 2 and nm == 2 and ng > 1 and rows % 16 == 0:
        mine = jnp.transpose(modes.reshape(2, -1, width), (0, 2, 1))
        theirs = shifted(mine, "ma", 1)
        front = lax.axis_index("ma") == 0
        left = jnp.concatenate(
            [jnp.where(front, mine, theirs), jnp.where(front, theirs, mine)], axis=1
        )
        return reduce_projections(left, right_x, right_y)
    left = lax.all_gather(modes.reshape(2, -1, width), "ma", axis=2, tiled=True)
    outputs = []
    for right in (right_x, right_y):
        real_out = contract(left[0], right[0]) + contract(left[1], right[1])
        imag_out = contract(left[0], right[1]) - contract(left[1], right[0])
        outputs.append(jnp.stack([real_out, imag_out]))
    partial_terms = jnp.stack(outputs)
    across_x = lax.psum_scatter(partial_terms, "gx", scatter_dimension=2, tiled=True)
    return lax.psum_scatter(across_x, "gy", scatter_dimension=2, tiled=True)


def solution(mesh):
    return jax.shard_map(
        local,
        mesh=mesh,
        in_specs=(
            P("cuts", "gx", "gy", None, None, "ma"),
            P("cuts", None, None, "gx", "gy", None),
            P("cuts", None, None, "gx", "gy", None),
        ),
        out_specs=P("cuts", None, ("gx", "gy"), "ma"),
        check_vma=False,
    )
```

```python
import functools

import jax
import jax.numpy as jnp
from jax import lax
from jax.experimental import pallas as pl
from jax.experimental.pallas import tpu as pltpu
from jax.sharding import PartitionSpec as P

MESH = pl.DeviceIdType.MESH


def shifted(block, axis, distance):
    devices = range(lax.axis_size(axis))
    route = [((i - distance) % len(devices), i) for i in devices]
    return lax.ppermute(block, axis, route)


def apply_link(linkage, field, dagger):
    link_real = linkage[0].astype(jnp.float32)
    link_imag = linkage[1].astype(jnp.float32)
    factor = -1.0 if dagger else 1.0
    real_rows = []
    imag_rows = []
    for row in range(3):
        real_acc = None
        imag_acc = None
        for col in range(3):
            if dagger:
                coef_real = link_real[col, row][..., None]
                coef_imag = link_imag[col, row][..., None]
            else:
                coef_real = link_real[row, col][..., None]
                coef_imag = link_imag[row, col][..., None]
            field_real = field[0, col]
            field_imag = field[1, col]
            term_real = coef_real * field_real - factor * coef_imag * field_imag
            term_imag = coef_real * field_imag + factor * coef_imag * field_real
            real_acc = term_real if real_acc is None else real_acc + term_real
            imag_acc = term_imag if imag_acc is None else imag_acc + term_imag
        real_rows.append(real_acc)
        imag_rows.append(imag_acc)
    return jnp.stack([jnp.stack(real_rows), jnp.stack(imag_rows)])


def contract(left, right_side):
    return lax.dot_general(
        left, right_side, (((0,), (0,)), ((), ())), preferred_element_type=jnp.float32
    )


def linked(coefs, real, imag, dagger):
    shape = real[0].shape
    outs_real, outs_imag = [], []
    for row in range(3):
        acc_real = acc_imag = None
        for col in range(3):
            k = 3 * col + row if dagger else 3 * row + col
            cr = jnp.broadcast_to(coefs[:, k : k + 1], shape)
            ci = jnp.broadcast_to(coefs[:, 9 + k : 10 + k], shape)
            if dagger:
                term_real = cr * real[col] + ci * imag[col]
                term_imag = cr * imag[col] - ci * real[col]
            else:
                term_real = cr * real[col] - ci * imag[col]
                term_imag = cr * imag[col] + ci * real[col]
            acc_real = term_real if acc_real is None else acc_real + term_real
            acc_imag = term_imag if acc_imag is None else acc_imag + term_imag
        outs_real.append(acc_real)
        outs_imag.append(acc_imag)
    return outs_real + outs_imag


def fused_kernel(nx, v_ref, vt_ref, cx_ref, cy_ref, ce_ref, out_ref,
                 left, rx, ry, wx, fy, wy, hup, hlo, chx, chy, ysend, yrecv,
                 own, xsend, xrecv, zsend, zrecv,
                 hs_sem, hr_sem, l_sem, xs_sem, xr_sem, zs_sem, zr_sem):
    gx = lax.axis_index("gx")
    gy = lax.axis_index("gy")
    ma = lax.axis_index("ma")
    other = 1 - gy
    rows = out_ref.shape[2]
    planes, sites, width = v_ref.shape[2:]
    zdim = ce_ref.shape[1]
    f32 = jnp.float32
    tile = 16
    up, down = lax.rem(gx + 1, nx), lax.rem(gx + nx - 1, nx)

    barrier = pltpu.get_barrier_semaphore()
    for off in range(1, nx):
        pl.semaphore_signal(
            barrier, inc=1, device_id={"gx": lax.rem(gx + off, nx)}, device_id_type=MESH
        )
    pl.semaphore_signal(barrier, inc=1, device_id={"gy": other}, device_id_type=MESH)
    pl.semaphore_signal(barrier, inc=1, device_id={"ma": 1 - ma}, device_id_type=MESH)
    pl.semaphore_wait(barrier, nx + 1)

    def send(i, src, dst, target):
        copy = pltpu.make_async_remote_copy(
            src_ref=src, dst_ref=dst, send_sem=hs_sem.at[i], recv_sem=hr_sem.at[i],
            device_id=target, device_id_type=MESH,
        )
        copy.start()
        return copy

    copy_down = send(0, v_ref.at[:, :, 0], hup, {"gx": down})
    copy_up = send(1, v_ref.at[:, :, planes - 1], hlo, {"gx": up})
    copy_cx = send(2, cx_ref.at[planes - 1], chx, {"gx": up})
    copy_cy = send(3, ce_ref, chy, {"gy": other})
    copy_vt = send(4, vt_ref, left.at[ma], {"ma": 1 - ma})
    copy_own = pltpu.make_async_copy(vt_ref, left.at[ma], l_sem)
    copy_own.start()

    def part(t):
        return pl.ds(t * tile, tile)

    def load(getter, t):
        real = [getter(0, c, t).astype(f32) for c in range(3)]
        imag = [getter(1, c, t).astype(f32) for c in range(3)]
        return real, imag

    def back_x(coefs, getter, slot, t):
        values = linked(coefs, *load(getter, t), True)
        for i in range(6):
            wx[slot, i, part(t)] = values[i]

    def fore_x(x, coefs, getter, edge_slot, t):
        values = linked(coefs, *load(getter, t), False)
        for i in range(6):
            value = (values[i] - wx[x, i, part(t)]).astype(rx.dtype)
            rx[i // 3, i % 3, x, part(t)] = value
            wide = value.astype(f32)
            if t == 0:
                ysend[0, edge_slot, i] = wide[:zdim].astype(ysend.dtype)
            if t == sites // tile - 1:
                ysend[1, edge_slot, i] = wide[tile - zdim :].astype(ysend.dtype)

    def plane(x):
        return lambda p, c, t: v_ref[p, c, x, part(t)]

    tiles = range(sites // tile)
    for t in tiles:
        back_x(cx_ref[0, part(t)], plane(0), 1, t)

    def inner(x, carry):
        for t in tiles:
            coefs = cx_ref[x, part(t)]
            back_x(coefs, plane(x), x + 1, t)
            fore_x(x, coefs, plane(x + 1), x - 1, t)
        return carry

    lax.fori_loop(1, planes - 1, inner, 0)
    inner_edges = planes - 2
    copies_y = [
        send(5 + s, ysend.at[s, pl.ds(0, inner_edges)], yrecv.at[s, pl.ds(0, inner_edges)],
             {"gy": other})
        for s in range(2)
    ]
    copy_cx.wait()
    copy_up.wait()
    for t in tiles:
        back_x(chx[part(t)], lambda p, c, t: hlo[p, c, part(t)], 0, t)
        fore_x(0, cx_ref[0, part(t)], plane(1), inner_edges, t)
    copy_down.wait()
    for t in tiles:
        fore_x(planes - 1, cx_ref[planes - 1, part(t)],
               lambda p, c, t: hup[p, c, part(t)], inner_edges + 1, t)
    copies_y += [
        send(7 + s, ysend.at[s, pl.ds(inner_edges, 2)], yrecv.at[s, pl.ds(inner_edges, 2)],
             {"gy": other})
        for s in range(2)
    ]
    copy_vt.wait()
    copy_own.wait()

    offsets = sorted(range(1, nx), key=lambda o: -min(o, nx - o)) + [0]
    rights = (rx, ry)
    modes = left.shape[2]
    depth = left.shape[3]
    dot = functools.partial(jnp.dot, preferred_element_type=f32)
    x_copies, z_copies = {}, {}

    def project(k, d):
        c = 2 * k + d
        base = lax.rem(gx + offsets[k], nx) * (2 * rows)
        half = base // modes
        start = pl.multiple_of(base - half * modes, 2 * rows)
        left_real = left[half, 0, pl.ds(start, 2 * rows), :]
        left_imag = left[half, 1, pl.ds(start, 2 * rows), :]
        right_real = rights[d][0].reshape(depth, width)
        right_imag = rights[d][1].reshape(depth, width)
        real = dot(left_real, right_real) + dot(left_imag, right_imag)
        imag = dot(left_real, right_imag) - dot(left_imag, right_real)
        first = jnp.stack([real[:rows], imag[:rows]])
        second = jnp.stack([real[rows:], imag[rows:]])
        own[c] = jnp.where(gy == 0, first, second)
        xsend[c] = jnp.where(gy == 0, second, first).astype(xsend.dtype)
        copy = pltpu.make_async_remote_copy(
            src_ref=xsend.at[c], dst_ref=xrecv.at[c],
            send_sem=xs_sem.at[c], recv_sem=xr_sem.at[c],
            device_id={"gy": other}, device_id_type=MESH,
        )
        copy.start()
        x_copies[c] = copy

    def pass_on(k, d):
        c = 2 * k + d
        x_copies[c].wait()
        total = own[c] + xrecv[c].astype(f32)
        if offsets[k] == 0:
            own[c] = total
            return
        zsend[c] = total.astype(zsend.dtype)
        copy = pltpu.make_async_remote_copy(
            src_ref=zsend.at[c], dst_ref=zrecv.at[c],
            send_sem=zs_sem.at[c], recv_sem=zr_sem.at[c],
            device_id={"gx": lax.rem(gx + offsets[k], nx)}, device_id_type=MESH,
        )
        copy.start()
        z_copies[c] = copy

    for k in range(nx):
        project(k, 0)

    copy_cy.wait()
    for copy in copies_y:
        copy.wait()
    pad = 8

    def y_plane(x, slot):
        for i in range(6):
            fy[i, pad : pad + sites] = rx[i // 3, i % 3, x].astype(f32)
            fy[i, pad + sites : pad + sites + zdim] = yrecv[0, slot, i].astype(f32)
        low = [yrecv[1, slot, i].astype(f32) for i in range(6)]
        values = linked(chy[x], low[:3], low[3:], True)
        for i in range(6):
            wy[i, pad - zdim : pad] = values[i]
        for t in tiles:
            coefs = cy_ref[x, part(t)]
            here = [fy[i, pad + t * tile : pad + (t + 1) * tile] for i in range(6)]
            values = linked(coefs, here[:3], here[3:], True)
            for i in range(6):
                wy[i, pad + t * tile : pad + (t + 1) * tile] = values[i]
            ahead = [fy[i, pad + zdim + t * tile : pad + zdim + (t + 1) * tile] for i in range(6)]
            values = linked(coefs, ahead[:3], ahead[3:], False)
            for i in range(6):
                behind = wy[i, pad - zdim + t * tile : pad - zdim + (t + 1) * tile]
                ry[i // 3, i % 3, x, part(t)] = (values[i] - behind).astype(ry.dtype)

    def y_loop(x, carry):
        y_plane(x, jnp.where(x == 0, inner_edges, jnp.where(x == planes - 1, inner_edges + 1, x - 1)))
        return carry

    lax.fori_loop(0, planes, y_loop, 0)

    for k in range(nx):
        project(k, 1)
        pass_on(k, 0)
    for k in range(nx):
        pass_on(k, 1)
    last = 2 * (nx - 1)
    for d in range(2):
        total = own[last + d]
        for k in range(nx - 1):
            z_copies[2 * k + d].wait()
            total = total + zrecv[2 * k + d].astype(f32)
        out_ref[d] = total


def fused(eigen_modes, links_first, links_second):
    nx = lax.axis_size("gx")
    ny = lax.axis_size("gy")
    nm = lax.axis_size("ma")
    _, planes, ysize, zdim, _, width = eigen_modes.shape
    sites = ysize * zdim
    depth = 3 * planes * sites
    v = jnp.transpose(eigen_modes, (0, 4, 1, 2, 3, 5)).reshape(2, 3, planes, sites, width)
    vt = jnp.transpose(eigen_modes, (0, 5, 4, 1, 2, 3)).reshape(2, width, depth)

    def coefs(links):
        return jnp.transpose(links, (3, 4, 5, 0, 1, 2)).reshape(planes, sites, 18).astype(jnp.float32)

    cx = coefs(links_first)
    cy = coefs(links_second)
    ce = cy[:, sites - zdim :]
    rows = width * nm // (nx * ny)
    count = 2 * nx
    bf16, f32 = jnp.bfloat16, jnp.float32
    vmem = pl.BlockSpec(memory_space=pltpu.VMEM)
    chunk = (2, rows, width)
    edges = 2 * 2
    return pl.pallas_call(
        functools.partial(fused_kernel, nx),
        out_shape=jax.ShapeDtypeStruct((2, 2, rows, width), f32),
        in_specs=[vmem] * 5,
        out_specs=vmem,
        scratch_shapes=[
            pltpu.VMEM((nm, 2, width, depth), bf16),
            pltpu.VMEM((2, 3, planes, sites, width), bf16),
            pltpu.VMEM((2, 3, planes, sites, width), bf16),
            pltpu.VMEM((planes, 6, sites, width), f32),
            pltpu.VMEM((6, sites + 16, width), f32),
            pltpu.VMEM((6, sites + 16, width), f32),
            pltpu.VMEM((2, 3, sites, width), bf16),
            pltpu.VMEM((2, 3, sites, width), bf16),
            pltpu.VMEM((sites, 18), f32),
            pltpu.VMEM((planes, zdim, 18), f32),
            pltpu.VMEM((2, planes, 6, zdim, width), bf16),
            pltpu.VMEM((2, planes, 6, zdim, width), bf16),
            pltpu.VMEM((count,) + chunk, f32),
            pltpu.VMEM((count,) + chunk, bf16),
            pltpu.VMEM((count,) + chunk, bf16),
            pltpu.VMEM((count - 2,) + chunk, bf16),
            pltpu.VMEM((count - 2,) + chunk, bf16),
            pltpu.SemaphoreType.DMA((9,)),
            pltpu.SemaphoreType.DMA((9,)),
            pltpu.SemaphoreType.DMA,
            pltpu.SemaphoreType.DMA((count,)),
            pltpu.SemaphoreType.DMA((count,)),
            pltpu.SemaphoreType.DMA((count - 2,)),
            pltpu.SemaphoreType.DMA((count - 2,)),
        ],
        compiler_params=pltpu.CompilerParams(
            collective_id=0, has_side_effects=True, vmem_limit_bytes=56 * 1024 * 1024
        ),
    )(v, vt, cx, cy, ce)


def local(eigen_modes, links_first, links_second):
    width = eigen_modes.shape[5]
    ng, ny, nm = lax.axis_size("gx"), lax.axis_size("gy"), lax.axis_size("ma")
    sites = eigen_modes.shape[2] * eigen_modes.shape[3]
    rows = width * nm // (ng * ny)
    aligned = rows % 16 == 0 and width % (2 * rows) == 0 and sites % 16 == 0
    if ny == 2 and nm == 2 and ng > 1 and aligned and eigen_modes.shape[1] > 2:
        return fused(eigen_modes, links_first, links_second)
    modes = jnp.transpose(eigen_modes, (0, 4, 1, 2, 3, 5))
    upper = shifted(modes[:, :, :1], "gx", -1)
    lower = shifted(modes[:, :, -1:], "gx", 1)
    lower_links = shifted(links_first[:, :, :, -1:], "gx", 1)
    lower_links_y = shifted(links_second[:, :, :, :, -1:], "gy", 1)
    field = modes.astype(jnp.float32)
    forward = jnp.concatenate([modes[:, :, 1:], upper], axis=2).astype(jnp.float32)
    linked = apply_link(links_first[:, :, :, :-1], field[:, :, :-1], True)
    behind = apply_link(lower_links, lower.astype(jnp.float32), True)
    backward = jnp.concatenate([behind, linked], axis=2)
    disp_x = (apply_link(links_first, forward, False) - backward).astype(jnp.bfloat16)
    upper_row = shifted(disp_x[:, :, :, :1], "gy", -1)
    lower_row = shifted(disp_x[:, :, :, -1:], "gy", 1)
    forward_y = jnp.concatenate([disp_x[:, :, :, 1:], upper_row], axis=3).astype(jnp.float32)
    linked_y = apply_link(links_second[:, :, :, :, :-1], disp_x[:, :, :, :-1].astype(jnp.float32), True)
    behind_y = apply_link(lower_links_y, lower_row.astype(jnp.float32), True)
    backward_y = jnp.concatenate([behind_y, linked_y], axis=3)
    disp_xy = (apply_link(links_second, forward_y, False) - backward_y).astype(jnp.bfloat16)
    right_x = disp_x.reshape(2, -1, width)
    right_y = disp_xy.reshape(2, -1, width)
    left = lax.all_gather(modes.reshape(2, -1, width), "ma", axis=2, tiled=True)
    outputs = []
    for right in (right_x, right_y):
        real_out = contract(left[0], right[0]) + contract(left[1], right[1])
        imag_out = contract(left[0], right[1]) - contract(left[1], right[0])
        outputs.append(jnp.stack([real_out, imag_out]))
    partial_terms = jnp.stack(outputs)
    across_x = lax.psum_scatter(partial_terms, "gx", scatter_dimension=2, tiled=True)
    return lax.psum_scatter(across_x, "gy", scatter_dimension=2, tiled=True)


def solution(mesh):
    return jax.shard_map(
        local,
        mesh=mesh,
        in_specs=(
            P("cuts", "gx", "gy", None, None, "ma"),
            P("cuts", None, None, "gx", "gy", None),
            P("cuts", None, None, "gx", "gy", None),
        ),
        out_specs=P("cuts", None, ("gx", "gy"), "ma"),
        check_vma=False,
    )
```

```python
import functools

import jax
import jax.numpy as jnp
from jax import lax
from jax.experimental import pallas as pl
from jax.experimental.pallas import tpu as pltpu
from jax.sharding import PartitionSpec as P

MESH = pl.DeviceIdType.MESH


def shifted(block, axis, distance):
    devices = range(lax.axis_size(axis))
    route = [((i - distance) % len(devices), i) for i in devices]
    return lax.ppermute(block, axis, route)


def apply_link(linkage, field, dagger):
    link_real = linkage[0].astype(jnp.float32)
    link_imag = linkage[1].astype(jnp.float32)
    factor = -1.0 if dagger else 1.0
    real_rows = []
    imag_rows = []
    for row in range(3):
        real_acc = None
        imag_acc = None
        for col in range(3):
            if dagger:
                coef_real = link_real[col, row][..., None]
                coef_imag = link_imag[col, row][..., None]
            else:
                coef_real = link_real[row, col][..., None]
                coef_imag = link_imag[row, col][..., None]
            field_real = field[0, col]
            field_imag = field[1, col]
            term_real = coef_real * field_real - factor * coef_imag * field_imag
            term_imag = coef_real * field_imag + factor * coef_imag * field_real
            real_acc = term_real if real_acc is None else real_acc + term_real
            imag_acc = term_imag if imag_acc is None else imag_acc + term_imag
        real_rows.append(real_acc)
        imag_rows.append(imag_acc)
    return jnp.stack([jnp.stack(real_rows), jnp.stack(imag_rows)])


def contract(left, right_side):
    return lax.dot_general(
        left, right_side, (((0,), (0,)), ((), ())), preferred_element_type=jnp.float32
    )


def linked(coefs, real, imag, dagger, first=0):
    shape = real[0].shape
    outs_real, outs_imag = [], []
    for row in range(3):
        acc_real = acc_imag = None
        for col in range(3):
            k = first + (3 * col + row if dagger else 3 * row + col)
            cr = jnp.broadcast_to(coefs[:, k : k + 1], shape)
            ci = jnp.broadcast_to(coefs[:, 9 + k : 10 + k], shape)
            if dagger:
                term_real = cr * real[col] + ci * imag[col]
                term_imag = cr * imag[col] - ci * real[col]
            else:
                term_real = cr * real[col] - ci * imag[col]
                term_imag = cr * imag[col] + ci * real[col]
            acc_real = term_real if acc_real is None else acc_real + term_real
            acc_imag = term_imag if acc_imag is None else acc_imag + term_imag
        outs_real.append(acc_real)
        outs_imag.append(acc_imag)
    return outs_real + outs_imag


def fused_kernel(nx, v_ref, cf_ref, out_ref,
                 left, vs, ce, hupraw, hloraw, rx, ry, wx, fy, wy, hup, hlo, chx, chy, ysend, yrecv,
                 own, xsend, xrecv, zsend, zrecv,
                 hs_sem, hr_sem, xs_sem, xr_sem, zs_sem, zr_sem):
    gx = lax.axis_index("gx")
    gy = lax.axis_index("gy")
    ma = lax.axis_index("ma")
    other = 1 - gy
    rows = out_ref.shape[2]
    _, _, planes, sites, width = vs.shape
    zdim = ce.shape[1]
    f32 = jnp.float32
    tile = 16
    up, down = lax.rem(gx + 1, nx), lax.rem(gx + nx - 1, nx)

    barrier = pltpu.get_barrier_semaphore()
    for off in range(1, nx):
        pl.semaphore_signal(
            barrier, inc=1, device_id={"gx": lax.rem(gx + off, nx)}, device_id_type=MESH
        )
    pl.semaphore_signal(barrier, inc=1, device_id={"gy": other}, device_id_type=MESH)
    pl.semaphore_signal(barrier, inc=1, device_id={"ma": 1 - ma}, device_id_type=MESH)
    pl.semaphore_wait(barrier, nx + 1)

    def send(i, src, dst, target):
        copy = pltpu.make_async_remote_copy(
            src_ref=src, dst_ref=dst, send_sem=hs_sem.at[i], recv_sem=hr_sem.at[i],
            device_id=target, device_id_type=MESH,
        )
        copy.start()
        return copy

    copy_up = send(1, v_ref.at[:, planes - 1], hloraw, {"gx": up})
    copy_cx = send(2, cf_ref.at[planes - 1], chx, {"gx": up})
    copy_down = send(0, v_ref.at[:, 0], hupraw, {"gx": down})
    for x in range(planes):
        ce[x] = cf_ref[x, sites - zdim :]

    def relay(x, carry):
        for p in range(2):
            for c in range(3):
                vs[p, c, x] = v_ref[p, x, :, c].reshape(sites, width)
        return carry

    lax.fori_loop(0, planes, relay, 0)
    copy_cy = send(3, ce, chy, {"gy": other})
    span = planes * sites
    for p in range(2):
        for c in range(3):
            left[ma, p, :, c * span : (c + 1) * span] = vs[p, c].reshape(span, width).T
    copy_vt = send(4, left.at[ma], left.at[ma], {"ma": 1 - ma})

    def part(t):
        return pl.ds(t * tile, tile)

    def load(getter, t):
        real = [getter(0, c, t).astype(f32) for c in range(3)]
        imag = [getter(1, c, t).astype(f32) for c in range(3)]
        return real, imag

    def back_x(coefs, getter, slot, t):
        values = linked(coefs, *load(getter, t), True)
        for i in range(6):
            wx[slot, i, part(t)] = values[i]

    def fore_x(x, coefs, getter, edge_slot, t):
        values = linked(coefs, *load(getter, t), False)
        for i in range(6):
            value = (values[i] - wx[x, i, part(t)]).astype(rx.dtype)
            rx[i // 3, i % 3, x, part(t)] = value
            wide = value.astype(f32)
            if t == 0:
                ysend[0, edge_slot, i] = wide[:zdim].astype(ysend.dtype)
            if t == sites // tile - 1:
                ysend[1, edge_slot, i] = wide[tile - zdim :].astype(ysend.dtype)

    def plane(x):
        return lambda p, c, t: vs[p, c, x, part(t)]

    tiles = range(sites // tile)
    for t in tiles:
        back_x(cf_ref[0, part(t)], plane(0), 1, t)

    def inner(x, carry):
        for t in tiles:
            coefs = cf_ref[x, part(t)]
            back_x(coefs, plane(x), x + 1, t)
            fore_x(x, coefs, plane(x + 1), x - 1, t)
        return carry

    lax.fori_loop(1, planes - 1, inner, 0)
    inner_edges = planes - 2
    copies_y = [
        send(5 + s, ysend.at[s, pl.ds(0, inner_edges)], yrecv.at[s, pl.ds(0, inner_edges)],
             {"gy": other})
        for s in range(2)
    ]
    copy_cx.wait()
    copy_up.wait()
    for p in range(2):
        for c in range(3):
            hlo[p, c] = hloraw[p, :, c].reshape(sites, width)
    for t in tiles:
        back_x(chx[part(t)], lambda p, c, t: hlo[p, c, part(t)], 0, t)
        fore_x(0, cf_ref[0, part(t)], plane(1), inner_edges, t)
    copy_down.wait()
    for p in range(2):
        for c in range(3):
            hup[p, c] = hupraw[p, :, c].reshape(sites, width)
    for t in tiles:
        fore_x(planes - 1, cf_ref[planes - 1, part(t)],
               lambda p, c, t: hup[p, c, part(t)], inner_edges + 1, t)
    copies_y += [
        send(7 + s, ysend.at[s, pl.ds(inner_edges, 2)], yrecv.at[s, pl.ds(inner_edges, 2)],
             {"gy": other})
        for s in range(2)
    ]
    copy_vt.wait()

    offsets = sorted(range(1, nx), key=lambda o: -min(o, nx - o)) + [0]
    rights = (rx, ry)
    modes = left.shape[2]
    depth = left.shape[3]
    dot = functools.partial(jnp.dot, preferred_element_type=f32)
    x_copies, z_copies = {}, {}

    def project(k, d):
        c = 2 * k + d
        base = lax.rem(gx + offsets[k], nx) * (2 * rows)
        half = base // modes
        start = pl.multiple_of(base - half * modes, 2 * rows)
        left_real = left[half, 0, pl.ds(start, 2 * rows), :]
        left_imag = left[half, 1, pl.ds(start, 2 * rows), :]
        right_real = rights[d][0].reshape(depth, width)
        right_imag = rights[d][1].reshape(depth, width)
        real = dot(left_real, right_real) + dot(left_imag, right_imag)
        imag = dot(left_real, right_imag) - dot(left_imag, right_real)
        first = jnp.stack([real[:rows], imag[:rows]])
        second = jnp.stack([real[rows:], imag[rows:]])
        own[c] = jnp.where(gy == 0, first, second)
        xsend[c] = jnp.where(gy == 0, second, first).astype(xsend.dtype)
        copy = pltpu.make_async_remote_copy(
            src_ref=xsend.at[c], dst_ref=xrecv.at[c],
            send_sem=xs_sem.at[c], recv_sem=xr_sem.at[c],
            device_id={"gy": other}, device_id_type=MESH,
        )
        copy.start()
        x_copies[c] = copy

    def pass_on(k, d):
        c = 2 * k + d
        x_copies[c].wait()
        total = own[c] + xrecv[c].astype(f32)
        if offsets[k] == 0:
            own[c] = total
            return
        zsend[c] = total.astype(zsend.dtype)
        copy = pltpu.make_async_remote_copy(
            src_ref=zsend.at[c], dst_ref=zrecv.at[c],
            send_sem=zs_sem.at[c], recv_sem=zr_sem.at[c],
            device_id={"gx": lax.rem(gx + offsets[k], nx)}, device_id_type=MESH,
        )
        copy.start()
        z_copies[c] = copy

    for k in range(nx):
        project(k, 0)

    copy_cy.wait()
    for copy in copies_y:
        copy.wait()
    pad = 8

    def y_plane(x, slot):
        for i in range(6):
            fy[i, pad : pad + sites] = rx[i // 3, i % 3, x].astype(f32)
            fy[i, pad + sites : pad + sites + zdim] = yrecv[0, slot, i].astype(f32)
        low = [yrecv[1, slot, i].astype(f32) for i in range(6)]
        values = linked(chy[x], low[:3], low[3:], True, 18)
        for i in range(6):
            wy[i, pad - zdim : pad] = values[i]
        for t in tiles:
            coefs = cf_ref[x, part(t)]
            here = [fy[i, pad + t * tile : pad + (t + 1) * tile] for i in range(6)]
            values = linked(coefs, here[:3], here[3:], True, 18)
            for i in range(6):
                wy[i, pad + t * tile : pad + (t + 1) * tile] = values[i]
            ahead = [fy[i, pad + zdim + t * tile : pad + zdim + (t + 1) * tile] for i in range(6)]
            values = linked(coefs, ahead[:3], ahead[3:], False, 18)
            for i in range(6):
                behind = wy[i, pad - zdim + t * tile : pad - zdim + (t + 1) * tile]
                ry[i // 3, i % 3, x, part(t)] = (values[i] - behind).astype(ry.dtype)

    def y_loop(x, carry):
        y_plane(x, jnp.where(x == 0, inner_edges, jnp.where(x == planes - 1, inner_edges + 1, x - 1)))
        return carry

    lax.fori_loop(0, planes, y_loop, 0)

    for k in range(nx):
        project(k, 1)
        pass_on(k, 0)
    for k in range(nx):
        pass_on(k, 1)
    last = 2 * (nx - 1)
    for d in range(2):
        total = own[last + d]
        for k in range(nx - 1):
            z_copies[2 * k + d].wait()
            total = total + zrecv[2 * k + d].astype(f32)
        out_ref[d] = total


def fused(eigen_modes, links_first, links_second):
    nx = lax.axis_size("gx")
    ny = lax.axis_size("gy")
    nm = lax.axis_size("ma")
    _, planes, ysize, zdim, _, width = eigen_modes.shape
    sites = ysize * zdim
    depth = 3 * planes * sites
    v = jnp.transpose(eigen_modes, (0, 1, 2, 4, 3, 5))
    links = jnp.stack([links_first, links_second])
    cf = jnp.transpose(links, (4, 5, 6, 0, 1, 2, 3)).reshape(planes, sites, 36)
    cf = cf.astype(jnp.float32)
    rows = width * nm // (nx * ny)
    count = 2 * nx
    bf16, f32 = jnp.bfloat16, jnp.float32
    vmem = pl.BlockSpec(memory_space=pltpu.VMEM)
    chunk = (2, rows, width)
    return pl.pallas_call(
        functools.partial(fused_kernel, nx),
        out_shape=jax.ShapeDtypeStruct((2, 2, rows, width), f32),
        in_specs=[vmem] * 2,
        out_specs=vmem,
        scratch_shapes=[
            pltpu.VMEM((nm, 2, width, depth), bf16),
            pltpu.VMEM((2, 3, planes, sites, width), bf16),
            pltpu.VMEM((planes, zdim, 36), f32),
            pltpu.VMEM((2, ysize, 3, zdim, width), bf16),
            pltpu.VMEM((2, ysize, 3, zdim, width), bf16),
            pltpu.VMEM((2, 3, planes, sites, width), bf16),
            pltpu.VMEM((2, 3, planes, sites, width), bf16),
            pltpu.VMEM((planes, 6, sites, width), f32),
            pltpu.VMEM((6, sites + 16, width), f32),
            pltpu.VMEM((6, sites + 16, width), f32),
            pltpu.VMEM((2, 3, sites, width), bf16),
            pltpu.VMEM((2, 3, sites, width), bf16),
            pltpu.VMEM((sites, 36), f32),
            pltpu.VMEM((planes, zdim, 36), f32),
            pltpu.VMEM((2, planes, 6, zdim, width), bf16),
            pltpu.VMEM((2, planes, 6, zdim, width), bf16),
            pltpu.VMEM((count,) + chunk, f32),
            pltpu.VMEM((count,) + chunk, bf16),
            pltpu.VMEM((count,) + chunk, bf16),
            pltpu.VMEM((count - 2,) + chunk, bf16),
            pltpu.VMEM((count - 2,) + chunk, bf16),
            pltpu.SemaphoreType.DMA((9,)),
            pltpu.SemaphoreType.DMA((9,)),
            pltpu.SemaphoreType.DMA((count,)),
            pltpu.SemaphoreType.DMA((count,)),
            pltpu.SemaphoreType.DMA((count - 2,)),
            pltpu.SemaphoreType.DMA((count - 2,)),
        ],
        compiler_params=pltpu.CompilerParams(
            collective_id=0, has_side_effects=True, vmem_limit_bytes=24 * 1024 * 1024
        ),
    )(v, cf)


def local(eigen_modes, links_first, links_second):
    width = eigen_modes.shape[5]
    ng, ny, nm = lax.axis_size("gx"), lax.axis_size("gy"), lax.axis_size("ma")
    sites = eigen_modes.shape[2] * eigen_modes.shape[3]
    rows = width * nm // (ng * ny)
    aligned = rows % 16 == 0 and width % (2 * rows) == 0 and sites % 16 == 0
    if ny == 2 and nm == 2 and ng > 1 and aligned and eigen_modes.shape[1] > 2:
        return fused(eigen_modes, links_first, links_second)
    modes = jnp.transpose(eigen_modes, (0, 4, 1, 2, 3, 5))
    upper = shifted(modes[:, :, :1], "gx", -1)
    lower = shifted(modes[:, :, -1:], "gx", 1)
    lower_links = shifted(links_first[:, :, :, -1:], "gx", 1)
    lower_links_y = shifted(links_second[:, :, :, :, -1:], "gy", 1)
    field = modes.astype(jnp.float32)
    forward = jnp.concatenate([modes[:, :, 1:], upper], axis=2).astype(jnp.float32)
    linked = apply_link(links_first[:, :, :, :-1], field[:, :, :-1], True)
    behind = apply_link(lower_links, lower.astype(jnp.float32), True)
    backward = jnp.concatenate([behind, linked], axis=2)
    disp_x = (apply_link(links_first, forward, False) - backward).astype(jnp.bfloat16)
    upper_row = shifted(disp_x[:, :, :, :1], "gy", -1)
    lower_row = shifted(disp_x[:, :, :, -1:], "gy", 1)
    forward_y = jnp.concatenate([disp_x[:, :, :, 1:], upper_row], axis=3).astype(jnp.float32)
    linked_y = apply_link(links_second[:, :, :, :, :-1], disp_x[:, :, :, :-1].astype(jnp.float32), True)
    behind_y = apply_link(lower_links_y, lower_row.astype(jnp.float32), True)
    backward_y = jnp.concatenate([behind_y, linked_y], axis=3)
    disp_xy = (apply_link(links_second, forward_y, False) - backward_y).astype(jnp.bfloat16)
    right_x = disp_x.reshape(2, -1, width)
    right_y = disp_xy.reshape(2, -1, width)
    left = lax.all_gather(modes.reshape(2, -1, width), "ma", axis=2, tiled=True)
    outputs = []
    for right in (right_x, right_y):
        real_out = contract(left[0], right[0]) + contract(left[1], right[1])
        imag_out = contract(left[0], right[1]) - contract(left[1], right[0])
        outputs.append(jnp.stack([real_out, imag_out]))
    partial_terms = jnp.stack(outputs)
    across_x = lax.psum_scatter(partial_terms, "gx", scatter_dimension=2, tiled=True)
    return lax.psum_scatter(across_x, "gy", scatter_dimension=2, tiled=True)


def solution(mesh):
    return jax.shard_map(
        local,
        mesh=mesh,
        in_specs=(
            P("cuts", "gx", "gy", None, None, "ma"),
            P("cuts", None, None, "gx", "gy", None),
            P("cuts", None, None, "gx", "gy", None),
        ),
        out_specs=P("cuts", None, ("gx", "gy"), "ma"),
        check_vma=False,
    )
```

```python
import functools

import jax
import jax.numpy as jnp
from jax import lax
from jax.experimental import pallas as pl
from jax.experimental.pallas import tpu as pltpu
from jax.sharding import PartitionSpec as P

MESH = pl.DeviceIdType.MESH


def shifted(block, axis, distance):
    devices = range(lax.axis_size(axis))
    route = [((i - distance) % len(devices), i) for i in devices]
    return lax.ppermute(block, axis, route)


def apply_link(linkage, field, dagger):
    link_real = linkage[0].astype(jnp.float32)
    link_imag = linkage[1].astype(jnp.float32)
    factor = -1.0 if dagger else 1.0
    real_rows = []
    imag_rows = []
    for row in range(3):
        real_acc = None
        imag_acc = None
        for col in range(3):
            if dagger:
                coef_real = link_real[col, row][..., None]
                coef_imag = link_imag[col, row][..., None]
            else:
                coef_real = link_real[row, col][..., None]
                coef_imag = link_imag[row, col][..., None]
            field_real = field[0, col]
            field_imag = field[1, col]
            term_real = coef_real * field_real - factor * coef_imag * field_imag
            term_imag = coef_real * field_imag + factor * coef_imag * field_real
            real_acc = term_real if real_acc is None else real_acc + term_real
            imag_acc = term_imag if imag_acc is None else imag_acc + term_imag
        real_rows.append(real_acc)
        imag_rows.append(imag_acc)
    return jnp.stack([jnp.stack(real_rows), jnp.stack(imag_rows)])


def contract(left, right_side):
    return lax.dot_general(
        left, right_side, (((0,), (0,)), ((), ())), preferred_element_type=jnp.float32
    )


def linked(coefs, real, imag, dagger):
    shape = real[0].shape
    outs_real, outs_imag = [], []
    for row in range(3):
        acc_real = acc_imag = None
        for col in range(3):
            k = 3 * col + row if dagger else 3 * row + col
            cr = jnp.broadcast_to(coefs[:, k : k + 1], shape)
            ci = jnp.broadcast_to(coefs[:, 9 + k : 10 + k], shape)
            if dagger:
                term_real = cr * real[col] + ci * imag[col]
                term_imag = cr * imag[col] - ci * real[col]
            else:
                term_real = cr * real[col] - ci * imag[col]
                term_imag = cr * imag[col] + ci * real[col]
            acc_real = term_real if acc_real is None else acc_real + term_real
            acc_imag = term_imag if acc_imag is None else acc_imag + term_imag
        outs_real.append(acc_real)
        outs_imag.append(acc_imag)
    return outs_real + outs_imag


def fused_kernel(nx, v_ref, l1_ref, l2_ref, out_ref,
                 left, vs, cf, cf2, ce, hupraw, hloraw, rx, ry, wx, fy, wy, hup, hlo, chx, chy, ysend, yrecv,
                 own, xsend, xrecv, zsend, zrecv,
                 hs_sem, hr_sem, xs_sem, xr_sem, zs_sem, zr_sem):
    gx = lax.axis_index("gx")
    gy = lax.axis_index("gy")
    ma = lax.axis_index("ma")
    other = 1 - gy
    rows = out_ref.shape[2]
    _, _, planes, sites, width = vs.shape
    zdim = ce.shape[1]
    f32 = jnp.float32
    tile = 16
    up, down = lax.rem(gx + 1, nx), lax.rem(gx + nx - 1, nx)

    barrier = pltpu.get_barrier_semaphore()
    for off in range(1, nx):
        pl.semaphore_signal(
            barrier, inc=1, device_id={"gx": lax.rem(gx + off, nx)}, device_id_type=MESH
        )
    pl.semaphore_signal(barrier, inc=1, device_id={"gy": other}, device_id_type=MESH)
    pl.semaphore_signal(barrier, inc=1, device_id={"ma": 1 - ma}, device_id_type=MESH)

    sel_row = lax.broadcasted_iota(jnp.int32, (sites, sites // zdim), 0)
    sel_col = lax.broadcasted_iota(jnp.int32, (sites, sites // zdim), 1)
    picks = [(sel_row == sel_col * zdim + z).astype(jnp.bfloat16) for z in range(zdim)]

    def relay(x, carry):
        for source, target in ((l1_ref, cf), (l2_ref, cf2)):
            raw = source[:, x].astype(f32)
            total = None
            for z in range(zdim):
                term = lax.dot_general(
                    picks[z], raw[:, z, :].astype(jnp.bfloat16),
                    (((1,), (1,)), ((), ())), preferred_element_type=f32,
                )
                total = term if total is None else total + term
            target[x] = total
            if source is l2_ref:
                ce[x] = total[sites - zdim :]
        for p in range(2):
            for c in range(3):
                vs[p, c, x] = v_ref[p, x, :, c].reshape(sites, width)
        return carry

    lax.fori_loop(0, planes, relay, 0)
    pl.semaphore_wait(barrier, nx + 1)

    def send(i, src, dst, target):
        copy = pltpu.make_async_remote_copy(
            src_ref=src, dst_ref=dst, send_sem=hs_sem.at[i], recv_sem=hr_sem.at[i],
            device_id=target, device_id_type=MESH,
        )
        copy.start()
        return copy

    copy_up = send(1, v_ref.at[:, planes - 1], hloraw, {"gx": up})
    copy_cx = send(2, cf.at[planes - 1], chx, {"gx": up})
    copy_down = send(0, v_ref.at[:, 0], hupraw, {"gx": down})
    copy_cy = send(3, ce, chy, {"gy": other})
    span = planes * sites
    for p in range(2):
        for c in range(3):
            left[ma, p, :, c * span : (c + 1) * span] = vs[p, c].reshape(span, width).T
    copy_vt = send(4, left.at[ma], left.at[ma], {"ma": 1 - ma})

    def part(t):
        return pl.ds(t * tile, tile)

    def load(getter, t):
        real = [getter(0, c, t).astype(f32) for c in range(3)]
        imag = [getter(1, c, t).astype(f32) for c in range(3)]
        return real, imag

    def back_x(coefs, getter, slot, t):
        values = linked(coefs, *load(getter, t), True)
        for i in range(6):
            wx[slot, i, part(t)] = values[i]

    def fore_x(x, coefs, getter, edge_slot, t):
        values = linked(coefs, *load(getter, t), False)
        for i in range(6):
            value = (values[i] - wx[x, i, part(t)]).astype(rx.dtype)
            rx[i // 3, i % 3, x, part(t)] = value
            wide = value.astype(f32)
            if t == 0:
                ysend[0, edge_slot, i] = wide[:zdim].astype(ysend.dtype)
            if t == sites // tile - 1:
                ysend[1, edge_slot, i] = wide[tile - zdim :].astype(ysend.dtype)

    def plane(x):
        return lambda p, c, t: vs[p, c, x, part(t)]

    tiles = range(sites // tile)
    for t in tiles:
        back_x(cf[0, part(t)], plane(0), 1, t)

    def inner(x, carry):
        for t in tiles:
            coefs = cf[x, part(t)]
            back_x(coefs, plane(x), x + 1, t)
            fore_x(x, coefs, plane(x + 1), x - 1, t)
        return carry

    lax.fori_loop(1, planes - 1, inner, 0)
    inner_edges = planes - 2
    copies_y = [
        send(5 + s, ysend.at[s, pl.ds(0, inner_edges)], yrecv.at[s, pl.ds(0, inner_edges)],
             {"gy": other})
        for s in range(2)
    ]
    copy_cx.wait()
    copy_up.wait()
    for p in range(2):
        for c in range(3):
            hlo[p, c] = hloraw[p, :, c].reshape(sites, width)
    for t in tiles:
        back_x(chx[part(t)], lambda p, c, t: hlo[p, c, part(t)], 0, t)
        fore_x(0, cf[0, part(t)], plane(1), inner_edges, t)
    copy_down.wait()
    for p in range(2):
        for c in range(3):
            hup[p, c] = hupraw[p, :, c].reshape(sites, width)
    for t in tiles:
        fore_x(planes - 1, cf[planes - 1, part(t)],
               lambda p, c, t: hup[p, c, part(t)], inner_edges + 1, t)
    copies_y += [
        send(7 + s, ysend.at[s, pl.ds(inner_edges, 2)], yrecv.at[s, pl.ds(inner_edges, 2)],
             {"gy": other})
        for s in range(2)
    ]
    copy_vt.wait()

    offsets = sorted(range(1, nx), key=lambda o: -min(o, nx - o)) + [0]
    rights = (rx, ry)
    modes = left.shape[2]
    depth = left.shape[3]
    dot = functools.partial(jnp.dot, preferred_element_type=f32)
    x_copies, z_copies = {}, {}

    def project(k, d):
        c = 2 * k + d
        base = lax.rem(gx + offsets[k], nx) * (2 * rows)
        half = base // modes
        start = pl.multiple_of(base - half * modes, 2 * rows)
        left_real = left[half, 0, pl.ds(start, 2 * rows), :]
        left_imag = left[half, 1, pl.ds(start, 2 * rows), :]
        right_real = rights[d][0].reshape(depth, width)
        right_imag = rights[d][1].reshape(depth, width)
        real = dot(left_real, right_real) + dot(left_imag, right_imag)
        imag = dot(left_real, right_imag) - dot(left_imag, right_real)
        first = jnp.stack([real[:rows], imag[:rows]])
        second = jnp.stack([real[rows:], imag[rows:]])
        own[c] = jnp.where(gy == 0, first, second)
        xsend[c] = jnp.where(gy == 0, second, first).astype(xsend.dtype)
        copy = pltpu.make_async_remote_copy(
            src_ref=xsend.at[c], dst_ref=xrecv.at[c],
            send_sem=xs_sem.at[c], recv_sem=xr_sem.at[c],
            device_id={"gy": other}, device_id_type=MESH,
        )
        copy.start()
        x_copies[c] = copy

    def pass_on(k, d):
        c = 2 * k + d
        x_copies[c].wait()
        total = own[c] + xrecv[c].astype(f32)
        if offsets[k] == 0:
            own[c] = total
            return
        zsend[c] = total.astype(zsend.dtype)
        copy = pltpu.make_async_remote_copy(
            src_ref=zsend.at[c], dst_ref=zrecv.at[c],
            send_sem=zs_sem.at[c], recv_sem=zr_sem.at[c],
            device_id={"gx": lax.rem(gx + offsets[k], nx)}, device_id_type=MESH,
        )
        copy.start()
        z_copies[c] = copy

    for k in range(nx):
        project(k, 0)

    copy_cy.wait()
    for copy in copies_y:
        copy.wait()
    pad = 8

    def y_plane(x, slot):
        for i in range(6):
            fy[i, pad : pad + sites] = rx[i // 3, i % 3, x].astype(f32)
            fy[i, pad + sites : pad + sites + zdim] = yrecv[0, slot, i].astype(f32)
        low = [yrecv[1, slot, i].astype(f32) for i in range(6)]
        values = linked(chy[x], low[:3], low[3:], True)
        for i in range(6):
            wy[i, pad - zdim : pad] = values[i]
        for t in tiles:
            coefs = cf2[x, part(t)]
            here = [fy[i, pad + t * tile : pad + (t + 1) * tile] for i in range(6)]
            values = linked(coefs, here[:3], here[3:], True)
            for i in range(6):
                wy[i, pad + t * tile : pad + (t + 1) * tile] = values[i]
            ahead = [fy[i, pad + zdim + t * tile : pad + zdim + (t + 1) * tile] for i in range(6)]
            values = linked(coefs, ahead[:3], ahead[3:], False)
            for i in range(6):
                behind = wy[i, pad - zdim + t * tile : pad - zdim + (t + 1) * tile]
                ry[i // 3, i % 3, x, part(t)] = (values[i] - behind).astype(ry.dtype)

    def y_loop(x, carry):
        y_plane(x, jnp.where(x == 0, inner_edges, jnp.where(x == planes - 1, inner_edges + 1, x - 1)))
        return carry

    lax.fori_loop(0, planes, y_loop, 0)

    for k in range(nx):
        project(k, 1)
        pass_on(k, 0)
    for k in range(nx):
        pass_on(k, 1)
    last = 2 * (nx - 1)
    for d in range(2):
        total = own[last + d]
        for k in range(nx - 1):
            z_copies[2 * k + d].wait()
            total = total + zrecv[2 * k + d].astype(f32)
        out_ref[d] = total


def fused(eigen_modes, links_first, links_second):
    nx = lax.axis_size("gx")
    ny = lax.axis_size("gy")
    nm = lax.axis_size("ma")
    _, planes, ysize, zdim, _, width = eigen_modes.shape
    sites = ysize * zdim
    depth = 3 * planes * sites
    v = jnp.transpose(eigen_modes, (0, 1, 2, 4, 3, 5))

    def raw(links):
        return jnp.transpose(links, (0, 1, 2, 3, 5, 4)).reshape(18, planes, zdim, ysize)

    rows = width * nm // (nx * ny)
    count = 2 * nx
    bf16, f32 = jnp.bfloat16, jnp.float32
    vmem = pl.BlockSpec(memory_space=pltpu.VMEM)
    chunk = (2, rows, width)
    return pl.pallas_call(
        functools.partial(fused_kernel, nx),
        out_shape=jax.ShapeDtypeStruct((2, 2, rows, width), f32),
        in_specs=[vmem] * 3,
        out_specs=vmem,
        scratch_shapes=[
            pltpu.VMEM((nm, 2, width, depth), bf16),
            pltpu.VMEM((2, 3, planes, sites, width), bf16),
            pltpu.VMEM((planes, sites, 18), f32),
            pltpu.VMEM((planes, sites, 18), f32),
            pltpu.VMEM((planes, zdim, 18), f32),
            pltpu.VMEM((2, ysize, 3, zdim, width), bf16),
            pltpu.VMEM((2, ysize, 3, zdim, width), bf16),
            pltpu.VMEM((2, 3, planes, sites, width), bf16),
            pltpu.VMEM((2, 3, planes, sites, width), bf16),
            pltpu.VMEM((planes, 6, sites, width), f32),
            pltpu.VMEM((6, sites + 16, width), f32),
            pltpu.VMEM((6, sites + 16, width), f32),
            pltpu.VMEM((2, 3, sites, width), bf16),
            pltpu.VMEM((2, 3, sites, width), bf16),
            pltpu.VMEM((sites, 18), f32),
            pltpu.VMEM((planes, zdim, 18), f32),
            pltpu.VMEM((2, planes, 6, zdim, width), bf16),
            pltpu.VMEM((2, planes, 6, zdim, width), bf16),
            pltpu.VMEM((count,) + chunk, f32),
            pltpu.VMEM((count,) + chunk, bf16),
            pltpu.VMEM((count,) + chunk, bf16),
            pltpu.VMEM((count - 2,) + chunk, bf16),
            pltpu.VMEM((count - 2,) + chunk, bf16),
            pltpu.SemaphoreType.DMA((9,)),
            pltpu.SemaphoreType.DMA((9,)),
            pltpu.SemaphoreType.DMA((count,)),
            pltpu.SemaphoreType.DMA((count,)),
            pltpu.SemaphoreType.DMA((count - 2,)),
            pltpu.SemaphoreType.DMA((count - 2,)),
        ],
        compiler_params=pltpu.CompilerParams(
            collective_id=0, has_side_effects=True, vmem_limit_bytes=24 * 1024 * 1024
        ),
    )(v, raw(links_first), raw(links_second))


def local(eigen_modes, links_first, links_second):
    width = eigen_modes.shape[5]
    ng, ny, nm = lax.axis_size("gx"), lax.axis_size("gy"), lax.axis_size("ma")
    sites = eigen_modes.shape[2] * eigen_modes.shape[3]
    rows = width * nm // (ng * ny)
    aligned = rows % 16 == 0 and width % (2 * rows) == 0 and sites % 16 == 0
    if ny == 2 and nm == 2 and ng > 1 and aligned and eigen_modes.shape[1] > 2:
        return fused(eigen_modes, links_first, links_second)
    modes = jnp.transpose(eigen_modes, (0, 4, 1, 2, 3, 5))
    upper = shifted(modes[:, :, :1], "gx", -1)
    lower = shifted(modes[:, :, -1:], "gx", 1)
    lower_links = shifted(links_first[:, :, :, -1:], "gx", 1)
    lower_links_y = shifted(links_second[:, :, :, :, -1:], "gy", 1)
    field = modes.astype(jnp.float32)
    forward = jnp.concatenate([modes[:, :, 1:], upper], axis=2).astype(jnp.float32)
    linked = apply_link(links_first[:, :, :, :-1], field[:, :, :-1], True)
    behind = apply_link(lower_links, lower.astype(jnp.float32), True)
    backward = jnp.concatenate([behind, linked], axis=2)
    disp_x = (apply_link(links_first, forward, False) - backward).astype(jnp.bfloat16)
    upper_row = shifted(disp_x[:, :, :, :1], "gy", -1)
    lower_row = shifted(disp_x[:, :, :, -1:], "gy", 1)
    forward_y = jnp.concatenate([disp_x[:, :, :, 1:], upper_row], axis=3).astype(jnp.float32)
    linked_y = apply_link(links_second[:, :, :, :, :-1], disp_x[:, :, :, :-1].astype(jnp.float32), True)
    behind_y = apply_link(lower_links_y, lower_row.astype(jnp.float32), True)
    backward_y = jnp.concatenate([behind_y, linked_y], axis=3)
    disp_xy = (apply_link(links_second, forward_y, False) - backward_y).astype(jnp.bfloat16)
    right_x = disp_x.reshape(2, -1, width)
    right_y = disp_xy.reshape(2, -1, width)
    left = lax.all_gather(modes.reshape(2, -1, width), "ma", axis=2, tiled=True)
    outputs = []
    for right in (right_x, right_y):
        real_out = contract(left[0], right[0]) + contract(left[1], right[1])
        imag_out = contract(left[0], right[1]) - contract(left[1], right[0])
        outputs.append(jnp.stack([real_out, imag_out]))
    partial_terms = jnp.stack(outputs)
    across_x = lax.psum_scatter(partial_terms, "gx", scatter_dimension=2, tiled=True)
    return lax.psum_scatter(across_x, "gy", scatter_dimension=2, tiled=True)


def solution(mesh):
    return jax.shard_map(
        local,
        mesh=mesh,
        in_specs=(
            P("cuts", "gx", "gy", None, None, "ma"),
            P("cuts", None, None, "gx", "gy", None),
            P("cuts", None, None, "gx", "gy", None),
        ),
        out_specs=P("cuts", None, ("gx", "gy"), "ma"),
        check_vma=False,
    )
```

```python
import functools

import jax
import jax.numpy as jnp
from jax import lax
from jax.experimental import pallas as pl
from jax.experimental.pallas import tpu as pltpu
from jax.sharding import PartitionSpec as P

MESH = pl.DeviceIdType.MESH


def shifted(block, axis, distance):
    devices = range(lax.axis_size(axis))
    route = [((i - distance) % len(devices), i) for i in devices]
    return lax.ppermute(block, axis, route)


def apply_link(linkage, field, dagger):
    link_real = linkage[0].astype(jnp.float32)
    link_imag = linkage[1].astype(jnp.float32)
    factor = -1.0 if dagger else 1.0
    real_rows = []
    imag_rows = []
    for row in range(3):
        real_acc = None
        imag_acc = None
        for col in range(3):
            if dagger:
                coef_real = link_real[col, row][..., None]
                coef_imag = link_imag[col, row][..., None]
            else:
                coef_real = link_real[row, col][..., None]
                coef_imag = link_imag[row, col][..., None]
            field_real = field[0, col]
            field_imag = field[1, col]
            term_real = coef_real * field_real - factor * coef_imag * field_imag
            term_imag = coef_real * field_imag + factor * coef_imag * field_real
            real_acc = term_real if real_acc is None else real_acc + term_real
            imag_acc = term_imag if imag_acc is None else imag_acc + term_imag
        real_rows.append(real_acc)
        imag_rows.append(imag_acc)
    return jnp.stack([jnp.stack(real_rows), jnp.stack(imag_rows)])


def contract(left, right_side):
    return lax.dot_general(
        left, right_side, (((0,), (0,)), ((), ())), preferred_element_type=jnp.float32
    )


def linked(coefs, real, imag, dagger):
    shape = real[0].shape
    outs_real, outs_imag = [], []
    for row in range(3):
        acc_real = acc_imag = None
        for col in range(3):
            k = 3 * col + row if dagger else 3 * row + col
            cr = jnp.broadcast_to(coefs[:, k : k + 1], shape)
            ci = jnp.broadcast_to(coefs[:, 9 + k : 10 + k], shape)
            if dagger:
                term_real = cr * real[col] + ci * imag[col]
                term_imag = cr * imag[col] - ci * real[col]
            else:
                term_real = cr * real[col] - ci * imag[col]
                term_imag = cr * imag[col] + ci * real[col]
            acc_real = term_real if acc_real is None else acc_real + term_real
            acc_imag = term_imag if acc_imag is None else acc_imag + term_imag
        outs_real.append(acc_real)
        outs_imag.append(acc_imag)
    return outs_real + outs_imag


def fused_kernel(nx, v_hbm, l1_hbm, l2_hbm, out_ref,
                 v_ref, l1_ref, l2_ref, left, vs, cf, cf2, ce, hupraw, hloraw, rx, ry, wx, fy, wy, hup, hlo, chx, chy, ysend, yrecv,
                 own, xsend, xrecv, zsend, zrecv,
                 in_sem, hs_sem, hr_sem, xs_sem, xr_sem, zs_sem, zr_sem):
    gx = lax.axis_index("gx")
    gy = lax.axis_index("gy")
    ma = lax.axis_index("ma")
    other = 1 - gy
    rows = out_ref.shape[2]
    _, _, planes, sites, width = vs.shape
    zdim = ce.shape[1]
    f32 = jnp.float32
    tile = 16
    up, down = lax.rem(gx + 1, nx), lax.rem(gx + nx - 1, nx)

    staged = [
        pltpu.make_async_copy(src, dst, in_sem.at[i])
        for i, (src, dst) in enumerate(((v_hbm, v_ref), (l1_hbm, l1_ref), (l2_hbm, l2_ref)))
    ]
    barrier = pltpu.get_barrier_semaphore()
    for off in range(1, nx):
        pl.semaphore_signal(
            barrier, inc=1, device_id={"gx": lax.rem(gx + off, nx)}, device_id_type=MESH
        )
    for copy in staged:
        copy.start()
    pl.semaphore_signal(barrier, inc=1, device_id={"gy": other}, device_id_type=MESH)
    pl.semaphore_signal(barrier, inc=1, device_id={"ma": 1 - ma}, device_id_type=MESH)

    sel_row = lax.broadcasted_iota(jnp.int32, (sites, sites // zdim), 0)
    sel_col = lax.broadcasted_iota(jnp.int32, (sites, sites // zdim), 1)
    picks = [(sel_row == sel_col * zdim + z).astype(jnp.bfloat16) for z in range(zdim)]

    def relay(x, carry):
        for source, target in ((l1_ref, cf), (l2_ref, cf2)):
            raw = source[:, x].astype(f32)
            total = None
            for z in range(zdim):
                term = lax.dot_general(
                    picks[z], raw[:, z, :].astype(jnp.bfloat16),
                    (((1,), (1,)), ((), ())), preferred_element_type=f32,
                )
                total = term if total is None else total + term
            target[x] = total
            if source is l2_ref:
                ce[x] = total[sites - zdim :]
        for p in range(2):
            for c in range(3):
                vs[p, c, x] = v_ref[p, x, :, c].reshape(sites, width)
        return carry

    for copy in staged:
        copy.wait()
    lax.fori_loop(0, planes, relay, 0)
    pl.semaphore_wait(barrier, nx + 1)

    def send(i, src, dst, target):
        copy = pltpu.make_async_remote_copy(
            src_ref=src, dst_ref=dst, send_sem=hs_sem.at[i], recv_sem=hr_sem.at[i],
            device_id=target, device_id_type=MESH,
        )
        copy.start()
        return copy

    copy_up = send(1, v_ref.at[:, planes - 1], hloraw, {"gx": up})
    copy_cx = send(2, cf.at[planes - 1], chx, {"gx": up})
    copy_down = send(0, v_ref.at[:, 0], hupraw, {"gx": down})
    copy_cy = send(3, ce, chy, {"gy": other})
    span = planes * sites
    for p in range(2):
        for c in range(3):
            left[ma, p, :, c * span : (c + 1) * span] = vs[p, c].reshape(span, width).T
    copy_vt = send(4, left.at[ma], left.at[ma], {"ma": 1 - ma})

    def part(t):
        return pl.ds(t * tile, tile)

    def load(getter, t):
        real = [getter(0, c, t).astype(f32) for c in range(3)]
        imag = [getter(1, c, t).astype(f32) for c in range(3)]
        return real, imag

    def back_x(coefs, getter, slot, t):
        values = linked(coefs, *load(getter, t), True)
        for i in range(6):
            wx[slot, i, part(t)] = values[i]

    def fore_x(x, coefs, getter, edge_slot, t):
        values = linked(coefs, *load(getter, t), False)
        for i in range(6):
            value = (values[i] - wx[x, i, part(t)]).astype(rx.dtype)
            rx[i // 3, i % 3, x, part(t)] = value
            wide = value.astype(f32)
            if t == 0:
                ysend[0, edge_slot, i] = wide[:zdim].astype(ysend.dtype)
            if t == sites // tile - 1:
                ysend[1, edge_slot, i] = wide[tile - zdim :].astype(ysend.dtype)

    def plane(x):
        return lambda p, c, t: vs[p, c, x, part(t)]

    tiles = range(sites // tile)
    for t in tiles:
        back_x(cf[0, part(t)], plane(0), 1, t)

    def inner(x, carry):
        for t in tiles:
            coefs = cf[x, part(t)]
            back_x(coefs, plane(x), x + 1, t)
            fore_x(x, coefs, plane(x + 1), x - 1, t)
        return carry

    lax.fori_loop(1, planes - 1, inner, 0)
    inner_edges = planes - 2
    copies_y = [
        send(5 + s, ysend.at[s, pl.ds(0, inner_edges)], yrecv.at[s, pl.ds(0, inner_edges)],
             {"gy": other})
        for s in range(2)
    ]
    copy_cx.wait()
    copy_up.wait()
    for p in range(2):
        for c in range(3):
            hlo[p, c] = hloraw[p, :, c].reshape(sites, width)
    for t in tiles:
        back_x(chx[part(t)], lambda p, c, t: hlo[p, c, part(t)], 0, t)
        fore_x(0, cf[0, part(t)], plane(1), inner_edges, t)
    copy_down.wait()
    for p in range(2):
        for c in range(3):
            hup[p, c] = hupraw[p, :, c].reshape(sites, width)
    for t in tiles:
        fore_x(planes - 1, cf[planes - 1, part(t)],
               lambda p, c, t: hup[p, c, part(t)], inner_edges + 1, t)
    copies_y += [
        send(7 + s, ysend.at[s, pl.ds(inner_edges, 2)], yrecv.at[s, pl.ds(inner_edges, 2)],
             {"gy": other})
        for s in range(2)
    ]
    copy_vt.wait()

    offsets = sorted(range(1, nx), key=lambda o: -min(o, nx - o)) + [0]
    rights = (rx, ry)
    modes = left.shape[2]
    depth = left.shape[3]
    dot = functools.partial(jnp.dot, preferred_element_type=f32)
    x_copies, z_copies = {}, {}

    def project(k, d):
        c = 2 * k + d
        base = lax.rem(gx + offsets[k], nx) * (2 * rows)
        half = base // modes
        start = pl.multiple_of(base - half * modes, 2 * rows)
        left_real = left[half, 0, pl.ds(start, 2 * rows), :]
        left_imag = left[half, 1, pl.ds(start, 2 * rows), :]
        right_real = rights[d][0].reshape(depth, width)
        right_imag = rights[d][1].reshape(depth, width)
        real = dot(left_real, right_real) + dot(left_imag, right_imag)
        imag = dot(left_real, right_imag) - dot(left_imag, right_real)
        first = jnp.stack([real[:rows], imag[:rows]])
        second = jnp.stack([real[rows:], imag[rows:]])
        own[c] = jnp.where(gy == 0, first, second)
        xsend[c] = jnp.where(gy == 0, second, first).astype(xsend.dtype)
        copy = pltpu.make_async_remote_copy(
            src_ref=xsend.at[c], dst_ref=xrecv.at[c],
            send_sem=xs_sem.at[c], recv_sem=xr_sem.at[c],
            device_id={"gy": other}, device_id_type=MESH,
        )
        copy.start()
        x_copies[c] = copy

    def pass_on(k, d):
        c = 2 * k + d
        x_copies[c].wait()
        total = own[c] + xrecv[c].astype(f32)
        if offsets[k] == 0:
            own[c] = total
            return
        zsend[c] = total.astype(zsend.dtype)
        copy = pltpu.make_async_remote_copy(
            src_ref=zsend.at[c], dst_ref=zrecv.at[c],
            send_sem=zs_sem.at[c], recv_sem=zr_sem.at[c],
            device_id={"gx": lax.rem(gx + offsets[k], nx)}, device_id_type=MESH,
        )
        copy.start()
        z_copies[c] = copy

    for k in range(nx):
        project(k, 0)

    copy_cy.wait()
    for copy in copies_y:
        copy.wait()
    pad = 8

    def y_plane(x, slot):
        for i in range(6):
            fy[i, pad : pad + sites] = rx[i // 3, i % 3, x].astype(f32)
            fy[i, pad + sites : pad + sites + zdim] = yrecv[0, slot, i].astype(f32)
        low = [yrecv[1, slot, i].astype(f32) for i in range(6)]
        values = linked(chy[x], low[:3], low[3:], True)
        for i in range(6):
            wy[i, pad - zdim : pad] = values[i]
        for t in tiles:
            coefs = cf2[x, part(t)]
            here = [fy[i, pad + t * tile : pad + (t + 1) * tile] for i in range(6)]
            values = linked(coefs, here[:3], here[3:], True)
            for i in range(6):
                wy[i, pad + t * tile : pad + (t + 1) * tile] = values[i]
            ahead = [fy[i, pad + zdim + t * tile : pad + zdim + (t + 1) * tile] for i in range(6)]
            values = linked(coefs, ahead[:3], ahead[3:], False)
            for i in range(6):
                behind = wy[i, pad - zdim + t * tile : pad - zdim + (t + 1) * tile]
                ry[i // 3, i % 3, x, part(t)] = (values[i] - behind).astype(ry.dtype)

    def y_loop(x, carry):
        y_plane(x, jnp.where(x == 0, inner_edges, jnp.where(x == planes - 1, inner_edges + 1, x - 1)))
        return carry

    lax.fori_loop(0, planes, y_loop, 0)

    for k in range(nx):
        project(k, 1)
        pass_on(k, 0)
    for k in range(nx):
        pass_on(k, 1)
    last = 2 * (nx - 1)
    for d in range(2):
        total = own[last + d]
        for k in range(nx - 1):
            z_copies[2 * k + d].wait()
            total = total + zrecv[2 * k + d].astype(f32)
        out_ref[d] = total


def fused(eigen_modes, links_first, links_second):
    nx = lax.axis_size("gx")
    ny = lax.axis_size("gy")
    nm = lax.axis_size("ma")
    _, planes, ysize, zdim, _, width = eigen_modes.shape
    sites = ysize * zdim
    depth = 3 * planes * sites
    v = jnp.transpose(eigen_modes, (0, 1, 2, 4, 3, 5))

    def raw(links):
        return jnp.transpose(links, (0, 1, 2, 3, 5, 4)).reshape(18, planes, zdim, ysize)

    rows = width * nm // (nx * ny)
    count = 2 * nx
    bf16, f32 = jnp.bfloat16, jnp.float32
    vmem = pl.BlockSpec(memory_space=pltpu.VMEM)
    chunk = (2, rows, width)
    return pl.pallas_call(
        functools.partial(fused_kernel, nx),
        out_shape=jax.ShapeDtypeStruct((2, 2, rows, width), f32),
        in_specs=[pl.BlockSpec(memory_space=pltpu.HBM)] * 3,
        out_specs=vmem,
        scratch_shapes=[
            pltpu.VMEM((2, planes, ysize, 3, zdim, width), bf16),
            pltpu.VMEM((18, planes, zdim, ysize), bf16),
            pltpu.VMEM((18, planes, zdim, ysize), bf16),
            pltpu.VMEM((nm, 2, width, depth), bf16),
            pltpu.VMEM((2, 3, planes, sites, width), bf16),
            pltpu.VMEM((planes, sites, 18), f32),
            pltpu.VMEM((planes, sites, 18), f32),
            pltpu.VMEM((planes, zdim, 18), f32),
            pltpu.VMEM((2, ysize, 3, zdim, width), bf16),
            pltpu.VMEM((2, ysize, 3, zdim, width), bf16),
            pltpu.VMEM((2, 3, planes, sites, width), bf16),
            pltpu.VMEM((2, 3, planes, sites, width), bf16),
            pltpu.VMEM((planes, 6, sites, width), f32),
            pltpu.VMEM((6, sites + 16, width), f32),
            pltpu.VMEM((6, sites + 16, width), f32),
            pltpu.VMEM((2, 3, sites, width), bf16),
            pltpu.VMEM((2, 3, sites, width), bf16),
            pltpu.VMEM((sites, 18), f32),
            pltpu.VMEM((planes, zdim, 18), f32),
            pltpu.VMEM((2, planes, 6, zdim, width), bf16),
            pltpu.VMEM((2, planes, 6, zdim, width), bf16),
            pltpu.VMEM((count,) + chunk, f32),
            pltpu.VMEM((count,) + chunk, bf16),
            pltpu.VMEM((count,) + chunk, bf16),
            pltpu.VMEM((count - 2,) + chunk, bf16),
            pltpu.VMEM((count - 2,) + chunk, bf16),
            pltpu.SemaphoreType.DMA((3,)),
            pltpu.SemaphoreType.DMA((9,)),
            pltpu.SemaphoreType.DMA((9,)),
            pltpu.SemaphoreType.DMA((count,)),
            pltpu.SemaphoreType.DMA((count,)),
            pltpu.SemaphoreType.DMA((count - 2,)),
            pltpu.SemaphoreType.DMA((count - 2,)),
        ],
        compiler_params=pltpu.CompilerParams(
            collective_id=0, has_side_effects=True, vmem_limit_bytes=24 * 1024 * 1024
        ),
    )(*[pltpu.with_memory_space_constraint(a, pltpu.HBM) for a in (v, raw(links_first), raw(links_second))])


def local(eigen_modes, links_first, links_second):
    width = eigen_modes.shape[5]
    ng, ny, nm = lax.axis_size("gx"), lax.axis_size("gy"), lax.axis_size("ma")
    sites = eigen_modes.shape[2] * eigen_modes.shape[3]
    rows = width * nm // (ng * ny)
    aligned = rows % 16 == 0 and width % (2 * rows) == 0 and sites % 16 == 0
    if ny == 2 and nm == 2 and ng > 1 and aligned and eigen_modes.shape[1] > 2:
        return fused(eigen_modes, links_first, links_second)
    modes = jnp.transpose(eigen_modes, (0, 4, 1, 2, 3, 5))
    upper = shifted(modes[:, :, :1], "gx", -1)
    lower = shifted(modes[:, :, -1:], "gx", 1)
    lower_links = shifted(links_first[:, :, :, -1:], "gx", 1)
    lower_links_y = shifted(links_second[:, :, :, :, -1:], "gy", 1)
    field = modes.astype(jnp.float32)
    forward = jnp.concatenate([modes[:, :, 1:], upper], axis=2).astype(jnp.float32)
    linked = apply_link(links_first[:, :, :, :-1], field[:, :, :-1], True)
    behind = apply_link(lower_links, lower.astype(jnp.float32), True)
    backward = jnp.concatenate([behind, linked], axis=2)
    disp_x = (apply_link(links_first, forward, False) - backward).astype(jnp.bfloat16)
    upper_row = shifted(disp_x[:, :, :, :1], "gy", -1)
    lower_row = shifted(disp_x[:, :, :, -1:], "gy", 1)
    forward_y = jnp.concatenate([disp_x[:, :, :, 1:], upper_row], axis=3).astype(jnp.float32)
    linked_y = apply_link(links_second[:, :, :, :, :-1], disp_x[:, :, :, :-1].astype(jnp.float32), True)
    behind_y = apply_link(lower_links_y, lower_row.astype(jnp.float32), True)
    backward_y = jnp.concatenate([behind_y, linked_y], axis=3)
    disp_xy = (apply_link(links_second, forward_y, False) - backward_y).astype(jnp.bfloat16)
    right_x = disp_x.reshape(2, -1, width)
    right_y = disp_xy.reshape(2, -1, width)
    left = lax.all_gather(modes.reshape(2, -1, width), "ma", axis=2, tiled=True)
    outputs = []
    for right in (right_x, right_y):
        real_out = contract(left[0], right[0]) + contract(left[1], right[1])
        imag_out = contract(left[0], right[1]) - contract(left[1], right[0])
        outputs.append(jnp.stack([real_out, imag_out]))
    partial_terms = jnp.stack(outputs)
    across_x = lax.psum_scatter(partial_terms, "gx", scatter_dimension=2, tiled=True)
    return lax.psum_scatter(across_x, "gy", scatter_dimension=2, tiled=True)


def solution(mesh):
    return jax.shard_map(
        local,
        mesh=mesh,
        in_specs=(
            P("cuts", "gx", "gy", None, None, "ma"),
            P("cuts", None, None, "gx", "gy", None),
            P("cuts", None, None, "gx", "gy", None),
        ),
        out_specs=P("cuts", None, ("gx", "gy"), "ma"),
        check_vma=False,
    )
```

```python
import functools

import jax
import jax.numpy as jnp
from jax import lax
from jax.experimental import pallas as pl
from jax.experimental.pallas import tpu as pltpu
from jax.sharding import PartitionSpec as P

MESH = pl.DeviceIdType.MESH


def shifted(block, axis, distance):
    devices = range(lax.axis_size(axis))
    route = [((i - distance) % len(devices), i) for i in devices]
    return lax.ppermute(block, axis, route)


def apply_link(linkage, field, dagger):
    link_real = linkage[0].astype(jnp.float32)
    link_imag = linkage[1].astype(jnp.float32)
    factor = -1.0 if dagger else 1.0
    real_rows = []
    imag_rows = []
    for row in range(3):
        real_acc = None
        imag_acc = None
        for col in range(3):
            if dagger:
                coef_real = link_real[col, row][..., None]
                coef_imag = link_imag[col, row][..., None]
            else:
                coef_real = link_real[row, col][..., None]
                coef_imag = link_imag[row, col][..., None]
            field_real = field[0, col]
            field_imag = field[1, col]
            term_real = coef_real * field_real - factor * coef_imag * field_imag
            term_imag = coef_real * field_imag + factor * coef_imag * field_real
            real_acc = term_real if real_acc is None else real_acc + term_real
            imag_acc = term_imag if imag_acc is None else imag_acc + term_imag
        real_rows.append(real_acc)
        imag_rows.append(imag_acc)
    return jnp.stack([jnp.stack(real_rows), jnp.stack(imag_rows)])


def contract(left, right_side):
    return lax.dot_general(
        left, right_side, (((0,), (0,)), ((), ())), preferred_element_type=jnp.float32
    )


def linked(coefs, real, imag, dagger):
    shape = real[0].shape
    outs_real, outs_imag = [], []
    for row in range(3):
        acc_real = acc_imag = None
        for col in range(3):
            k = 3 * col + row if dagger else 3 * row + col
            cr = jnp.broadcast_to(coefs[:, k : k + 1], shape)
            ci = jnp.broadcast_to(coefs[:, 9 + k : 10 + k], shape)
            if dagger:
                term_real = cr * real[col] + ci * imag[col]
                term_imag = cr * imag[col] - ci * real[col]
            else:
                term_real = cr * real[col] - ci * imag[col]
                term_imag = cr * imag[col] + ci * real[col]
            acc_real = term_real if acc_real is None else acc_real + term_real
            acc_imag = term_imag if acc_imag is None else acc_imag + term_imag
        outs_real.append(acc_real)
        outs_imag.append(acc_imag)
    return outs_real + outs_imag


def fused_kernel(nx, v_hbm, l1_hbm, l2_hbm, out_ref,
                 v_ref, l1_ref, l2_ref, left, vs, cf, cf2, ce, hupraw, hloraw, rx, ry, wx, fy, wy, hup, hlo, chx, chy, ysend, yrecv,
                 own, xsend, xrecv, zsend, zrecv,
                 in_sem, hs_sem, hr_sem, xs_sem, xr_sem, zs_sem, zr_sem):
    gx = lax.axis_index("gx")
    gy = lax.axis_index("gy")
    ma = lax.axis_index("ma")
    other = 1 - gy
    rows = out_ref.shape[2]
    _, _, planes, sites, width = vs.shape
    zdim = ce.shape[1]
    f32 = jnp.float32
    tile = 16
    up, down = lax.rem(gx + 1, nx), lax.rem(gx + nx - 1, nx)

    staged = [
        pltpu.make_async_copy(src, dst, in_sem.at[i])
        for i, (src, dst) in enumerate(((v_hbm, v_ref), (l1_hbm, l1_ref), (l2_hbm, l2_ref)))
    ]
    barrier = pltpu.get_barrier_semaphore()
    for neighbour in (up, down):
        pl.semaphore_signal(barrier, inc=1, device_id={"gx": neighbour}, device_id_type=MESH)
    for copy in staged:
        copy.start()
    pl.semaphore_signal(barrier, inc=1, device_id={"gy": other}, device_id_type=MESH)
    pl.semaphore_signal(barrier, inc=1, device_id={"ma": 1 - ma}, device_id_type=MESH)

    sel_row = lax.broadcasted_iota(jnp.int32, (sites, sites // zdim), 0)
    sel_col = lax.broadcasted_iota(jnp.int32, (sites, sites // zdim), 1)
    picks = [(sel_row == sel_col * zdim + z).astype(jnp.bfloat16) for z in range(zdim)]

    def relay(x, carry):
        for source, target in ((l1_ref, cf), (l2_ref, cf2)):
            raw = source[:, x].astype(f32)
            total = None
            for z in range(zdim):
                term = lax.dot_general(
                    picks[z], raw[:, z, :].astype(jnp.bfloat16),
                    (((1,), (1,)), ((), ())), preferred_element_type=f32,
                )
                total = term if total is None else total + term
            target[x] = total
            if source is l2_ref:
                ce[x] = total[sites - zdim :]
        for p in range(2):
            for c in range(3):
                vs[p, c, x] = v_ref[p, x, :, c].reshape(sites, width)
        return carry


    def send(i, src, dst, target):
        copy = pltpu.make_async_remote_copy(
            src_ref=src, dst_ref=dst, send_sem=hs_sem.at[i], recv_sem=hr_sem.at[i],
            device_id=target, device_id_type=MESH,
        )
        copy.start()
        return copy

    staged[0].wait()
    pl.semaphore_wait(barrier, 4)
    copy_up = send(1, v_ref.at[:, planes - 1], hloraw, {"gx": up})
    copy_down = send(0, v_ref.at[:, 0], hupraw, {"gx": down})
    for copy in staged[1:]:
        copy.wait()
    lax.fori_loop(0, planes, relay, 0)
    copy_cx = send(2, cf.at[planes - 1], chx, {"gx": up})
    copy_cy = send(3, ce, chy, {"gy": other})
    span = planes * sites
    for p in range(2):
        for c in range(3):
            left[ma, p, :, c * span : (c + 1) * span] = vs[p, c].reshape(span, width).T
    copy_vt = send(4, left.at[ma], left.at[ma], {"ma": 1 - ma})

    def part(t):
        return pl.ds(t * tile, tile)

    def load(getter, t):
        real = [getter(0, c, t).astype(f32) for c in range(3)]
        imag = [getter(1, c, t).astype(f32) for c in range(3)]
        return real, imag

    def back_x(coefs, getter, slot, t):
        values = linked(coefs, *load(getter, t), True)
        for i in range(6):
            wx[slot, i, part(t)] = values[i]

    def fore_x(x, coefs, getter, edge_slot, t):
        values = linked(coefs, *load(getter, t), False)
        for i in range(6):
            value = (values[i] - wx[x, i, part(t)]).astype(rx.dtype)
            rx[i // 3, i % 3, x, part(t)] = value
            wide = value.astype(f32)
            if t == 0:
                ysend[0, edge_slot, i] = wide[:zdim].astype(ysend.dtype)
            if t == sites // tile - 1:
                ysend[1, edge_slot, i] = wide[tile - zdim :].astype(ysend.dtype)

    def plane(x):
        return lambda p, c, t: vs[p, c, x, part(t)]

    tiles = range(sites // tile)
    for t in tiles:
        back_x(cf[0, part(t)], plane(0), 1, t)

    def inner(x, carry):
        for t in tiles:
            coefs = cf[x, part(t)]
            back_x(coefs, plane(x), x + 1, t)
            fore_x(x, coefs, plane(x + 1), x - 1, t)
        return carry

    lax.fori_loop(1, planes - 1, inner, 0)
    inner_edges = planes - 2
    copies_y = [
        send(5 + s, ysend.at[s, pl.ds(0, inner_edges)], yrecv.at[s, pl.ds(0, inner_edges)],
             {"gy": other})
        for s in range(2)
    ]
    copy_cx.wait()
    copy_up.wait()
    for p in range(2):
        for c in range(3):
            hlo[p, c] = hloraw[p, :, c].reshape(sites, width)
    for t in tiles:
        back_x(chx[part(t)], lambda p, c, t: hlo[p, c, part(t)], 0, t)
        fore_x(0, cf[0, part(t)], plane(1), inner_edges, t)
    copy_down.wait()
    for p in range(2):
        for c in range(3):
            hup[p, c] = hupraw[p, :, c].reshape(sites, width)
    for t in tiles:
        fore_x(planes - 1, cf[planes - 1, part(t)],
               lambda p, c, t: hup[p, c, part(t)], inner_edges + 1, t)
    copies_y += [
        send(7 + s, ysend.at[s, pl.ds(inner_edges, 2)], yrecv.at[s, pl.ds(inner_edges, 2)],
             {"gy": other})
        for s in range(2)
    ]
    copy_vt.wait()

    orders = [
        sorted(range(nx), key=lambda t: (t == g, -abs(t - g))) for g in range(nx)
    ]
    targets = []
    for step in range(nx):
        target = orders[0][step]
        for g in range(1, nx):
            target = jnp.where(gx == g, orders[g][step], target)
        targets.append(target)
    rights = (rx, ry)
    modes = left.shape[2]
    depth = left.shape[3]
    dot = functools.partial(jnp.dot, preferred_element_type=f32)
    x_copies, z_copies = {}, {}

    def project(k, d):
        c = 2 * k + d
        base = targets[k] * (2 * rows)
        half = base // modes
        start = pl.multiple_of(base - half * modes, 2 * rows)
        left_real = left[half, 0, pl.ds(start, 2 * rows), :]
        left_imag = left[half, 1, pl.ds(start, 2 * rows), :]
        right_real = rights[d][0].reshape(depth, width)
        right_imag = rights[d][1].reshape(depth, width)
        real = dot(left_real, right_real) + dot(left_imag, right_imag)
        imag = dot(left_real, right_imag) - dot(left_imag, right_real)
        first = jnp.stack([real[:rows], imag[:rows]])
        second = jnp.stack([real[rows:], imag[rows:]])
        own[c] = jnp.where(gy == 0, first, second)
        xsend[c] = jnp.where(gy == 0, second, first).astype(xsend.dtype)
        copy = pltpu.make_async_remote_copy(
            src_ref=xsend.at[c], dst_ref=xrecv.at[c],
            send_sem=xs_sem.at[c], recv_sem=xr_sem.at[c],
            device_id={"gy": other}, device_id_type=MESH,
        )
        copy.start()
        x_copies[c] = copy

    def arrived(c, side, slot):
        pltpu.make_async_remote_copy(
            src_ref=xsend.at[c], dst_ref=zrecv.at[side, slot],
            send_sem=xs_sem.at[c], recv_sem=zr_sem.at[side, slot],
            device_id={"gx": up}, device_id_type=MESH,
        ).wait_recv()
        own[c] = own[c] + zrecv[side, slot].astype(f32)

    def pass_on(k, d):
        c = 2 * k + d
        target = targets[k]
        slot = 2 * target + d
        x_copies[c].wait()
        own[c] = own[c] + xrecv[c].astype(f32)

        @pl.when(jnp.logical_and(gx > 0, target >= gx))
        def _():
            arrived(c, 0, slot)

        @pl.when(jnp.logical_and(gx < nx - 1, target <= gx))
        def _():
            arrived(c, 1, slot)

        if k == nx - 1:
            out_ref[d] = own[c]
            return
        right = target > gx
        side = jnp.where(right, 0, 1)
        zsend[c] = own[c].astype(zsend.dtype)
        copy = pltpu.make_async_remote_copy(
            src_ref=zsend.at[c], dst_ref=zrecv.at[side, slot],
            send_sem=zs_sem.at[c], recv_sem=zr_sem.at[side, slot],
            device_id={"gx": jnp.where(right, gx + 1, gx - 1)}, device_id_type=MESH,
        )
        copy.start()
        z_copies[c] = copy

    for k in range(nx):
        project(k, 0)

    copy_cy.wait()
    for copy in copies_y:
        copy.wait()
    pad = 8

    def y_plane(x, slot):
        for i in range(6):
            fy[i, pad : pad + sites] = rx[i // 3, i % 3, x].astype(f32)
            fy[i, pad + sites : pad + sites + zdim] = yrecv[0, slot, i].astype(f32)
        low = [yrecv[1, slot, i].astype(f32) for i in range(6)]
        values = linked(chy[x], low[:3], low[3:], True)
        for i in range(6):
            wy[i, pad - zdim : pad] = values[i]
        for t in tiles:
            coefs = cf2[x, part(t)]
            here = [fy[i, pad + t * tile : pad + (t + 1) * tile] for i in range(6)]
            values = linked(coefs, here[:3], here[3:], True)
            for i in range(6):
                wy[i, pad + t * tile : pad + (t + 1) * tile] = values[i]
            ahead = [fy[i, pad + zdim + t * tile : pad + zdim + (t + 1) * tile] for i in range(6)]
            values = linked(coefs, ahead[:3], ahead[3:], False)
            for i in range(6):
                behind = wy[i, pad - zdim + t * tile : pad - zdim + (t + 1) * tile]
                ry[i // 3, i % 3, x, part(t)] = (values[i] - behind).astype(ry.dtype)

    def y_loop(x, carry):
        y_plane(x, jnp.where(x == 0, inner_edges, jnp.where(x == planes - 1, inner_edges + 1, x - 1)))
        return carry

    lax.fori_loop(0, planes, y_loop, 0)

    for k in range(nx):
        project(k, 1)
        pass_on(k, 0)
    for k in range(nx):
        pass_on(k, 1)
    for c in z_copies:
        z_copies[c].wait_send()


def fused(eigen_modes, links_first, links_second):
    nx = lax.axis_size("gx")
    ny = lax.axis_size("gy")
    nm = lax.axis_size("ma")
    _, planes, ysize, zdim, _, width = eigen_modes.shape
    sites = ysize * zdim
    depth = 3 * planes * sites
    v = jnp.transpose(eigen_modes, (0, 1, 2, 4, 3, 5))

    def raw(links):
        return jnp.transpose(links, (0, 1, 2, 3, 5, 4)).reshape(18, planes, zdim, ysize)

    rows = width * nm // (nx * ny)
    count = 2 * nx
    bf16, f32 = jnp.bfloat16, jnp.float32
    vmem = pl.BlockSpec(memory_space=pltpu.VMEM)
    chunk = (2, rows, width)
    return pl.pallas_call(
        functools.partial(fused_kernel, nx),
        out_shape=jax.ShapeDtypeStruct((2, 2, rows, width), f32),
        in_specs=[pl.BlockSpec(memory_space=pltpu.HBM)] * 3,
        out_specs=vmem,
        scratch_shapes=[
            pltpu.VMEM((2, planes, ysize, 3, zdim, width), bf16),
            pltpu.VMEM((18, planes, zdim, ysize), bf16),
            pltpu.VMEM((18, planes, zdim, ysize), bf16),
            pltpu.VMEM((nm, 2, width, depth), bf16),
            pltpu.VMEM((2, 3, planes, sites, width), bf16),
            pltpu.VMEM((planes, sites, 18), f32),
            pltpu.VMEM((planes, sites, 18), f32),
            pltpu.VMEM((planes, zdim, 18), f32),
            pltpu.VMEM((2, ysize, 3, zdim, width), bf16),
            pltpu.VMEM((2, ysize, 3, zdim, width), bf16),
            pltpu.VMEM((2, 3, planes, sites, width), bf16),
            pltpu.VMEM((2, 3, planes, sites, width), bf16),
            pltpu.VMEM((planes, 6, sites, width), f32),
            pltpu.VMEM((6, sites + 16, width), f32),
            pltpu.VMEM((6, sites + 16, width), f32),
            pltpu.VMEM((2, 3, sites, width), bf16),
            pltpu.VMEM((2, 3, sites, width), bf16),
            pltpu.VMEM((sites, 18), f32),
            pltpu.VMEM((planes, zdim, 18), f32),
            pltpu.VMEM((2, planes, 6, zdim, width), bf16),
            pltpu.VMEM((2, planes, 6, zdim, width), bf16),
            pltpu.VMEM((count,) + chunk, f32),
            pltpu.VMEM((count,) + chunk, bf16),
            pltpu.VMEM((count,) + chunk, bf16),
            pltpu.VMEM((count - 2,) + chunk, bf16),
            pltpu.VMEM((2, count) + chunk, bf16),
            pltpu.SemaphoreType.DMA((3,)),
            pltpu.SemaphoreType.DMA((9,)),
            pltpu.SemaphoreType.DMA((9,)),
            pltpu.SemaphoreType.DMA((count,)),
            pltpu.SemaphoreType.DMA((count,)),
            pltpu.SemaphoreType.DMA((count - 2,)),
            pltpu.SemaphoreType.DMA((2, count)),
        ],
        compiler_params=pltpu.CompilerParams(
            collective_id=0, has_side_effects=True, vmem_limit_bytes=24 * 1024 * 1024
        ),
    )(*[pltpu.with_memory_space_constraint(a, pltpu.HBM) for a in (v, raw(links_first), raw(links_second))])


def local(eigen_modes, links_first, links_second):
    width = eigen_modes.shape[5]
    ng, ny, nm = lax.axis_size("gx"), lax.axis_size("gy"), lax.axis_size("ma")
    sites = eigen_modes.shape[2] * eigen_modes.shape[3]
    rows = width * nm // (ng * ny)
    aligned = rows % 16 == 0 and width % (2 * rows) == 0 and sites % 16 == 0
    if ny == 2 and nm == 2 and ng > 1 and aligned and eigen_modes.shape[1] > 2:
        return fused(eigen_modes, links_first, links_second)
    modes = jnp.transpose(eigen_modes, (0, 4, 1, 2, 3, 5))
    upper = shifted(modes[:, :, :1], "gx", -1)
    lower = shifted(modes[:, :, -1:], "gx", 1)
    lower_links = shifted(links_first[:, :, :, -1:], "gx", 1)
    lower_links_y = shifted(links_second[:, :, :, :, -1:], "gy", 1)
    field = modes.astype(jnp.float32)
    forward = jnp.concatenate([modes[:, :, 1:], upper], axis=2).astype(jnp.float32)
    linked = apply_link(links_first[:, :, :, :-1], field[:, :, :-1], True)
    behind = apply_link(lower_links, lower.astype(jnp.float32), True)
    backward = jnp.concatenate([behind, linked], axis=2)
    disp_x = (apply_link(links_first, forward, False) - backward).astype(jnp.bfloat16)
    upper_row = shifted(disp_x[:, :, :, :1], "gy", -1)
    lower_row = shifted(disp_x[:, :, :, -1:], "gy", 1)
    forward_y = jnp.concatenate([disp_x[:, :, :, 1:], upper_row], axis=3).astype(jnp.float32)
    linked_y = apply_link(links_second[:, :, :, :, :-1], disp_x[:, :, :, :-1].astype(jnp.float32), True)
    behind_y = apply_link(lower_links_y, lower_row.astype(jnp.float32), True)
    backward_y = jnp.concatenate([behind_y, linked_y], axis=3)
    disp_xy = (apply_link(links_second, forward_y, False) - backward_y).astype(jnp.bfloat16)
    right_x = disp_x.reshape(2, -1, width)
    right_y = disp_xy.reshape(2, -1, width)
    left = lax.all_gather(modes.reshape(2, -1, width), "ma", axis=2, tiled=True)
    outputs = []
    for right in (right_x, right_y):
        real_out = contract(left[0], right[0]) + contract(left[1], right[1])
        imag_out = contract(left[0], right[1]) - contract(left[1], right[0])
        outputs.append(jnp.stack([real_out, imag_out]))
    partial_terms = jnp.stack(outputs)
    across_x = lax.psum_scatter(partial_terms, "gx", scatter_dimension=2, tiled=True)
    return lax.psum_scatter(across_x, "gy", scatter_dimension=2, tiled=True)


def solution(mesh):
    return jax.shard_map(
        local,
        mesh=mesh,
        in_specs=(
            P("cuts", "gx", "gy", None, None, "ma"),
            P("cuts", None, None, "gx", "gy", None),
            P("cuts", None, None, "gx", "gy", None),
        ),
        out_specs=P("cuts", None, ("gx", "gy"), "ma"),
        check_vma=False,
    )
```

```python
import functools

import jax
import jax.numpy as jnp
from jax import lax
from jax.experimental import pallas as pl
from jax.experimental.pallas import tpu as pltpu
from jax.sharding import PartitionSpec as P

MESH = pl.DeviceIdType.MESH


def shifted(block, axis, distance):
    devices = range(lax.axis_size(axis))
    route = [((i - distance) % len(devices), i) for i in devices]
    return lax.ppermute(block, axis, route)


def apply_link(linkage, field, dagger):
    link_real = linkage[0].astype(jnp.float32)
    link_imag = linkage[1].astype(jnp.float32)
    factor = -1.0 if dagger else 1.0
    real_rows = []
    imag_rows = []
    for row in range(3):
        real_acc = None
        imag_acc = None
        for col in range(3):
            if dagger:
                coef_real = link_real[col, row][..., None]
                coef_imag = link_imag[col, row][..., None]
            else:
                coef_real = link_real[row, col][..., None]
                coef_imag = link_imag[row, col][..., None]
            field_real = field[0, col]
            field_imag = field[1, col]
            term_real = coef_real * field_real - factor * coef_imag * field_imag
            term_imag = coef_real * field_imag + factor * coef_imag * field_real
            real_acc = term_real if real_acc is None else real_acc + term_real
            imag_acc = term_imag if imag_acc is None else imag_acc + term_imag
        real_rows.append(real_acc)
        imag_rows.append(imag_acc)
    return jnp.stack([jnp.stack(real_rows), jnp.stack(imag_rows)])


def contract(left, right_side):
    return lax.dot_general(
        left, right_side, (((0,), (0,)), ((), ())), preferred_element_type=jnp.float32
    )


def linked(coefs, real, imag, dagger):
    shape = real[0].shape
    outs_real, outs_imag = [], []
    for row in range(3):
        acc_real = acc_imag = None
        for col in range(3):
            k = 3 * col + row if dagger else 3 * row + col
            cr = jnp.broadcast_to(coefs[:, k : k + 1], shape)
            ci = jnp.broadcast_to(coefs[:, 9 + k : 10 + k], shape)
            if dagger:
                term_real = cr * real[col] + ci * imag[col]
                term_imag = cr * imag[col] - ci * real[col]
            else:
                term_real = cr * real[col] - ci * imag[col]
                term_imag = cr * imag[col] + ci * real[col]
            acc_real = term_real if acc_real is None else acc_real + term_real
            acc_imag = term_imag if acc_imag is None else acc_imag + term_imag
        outs_real.append(acc_real)
        outs_imag.append(acc_imag)
    return outs_real + outs_imag


def fused_kernel(nx, v_hbm, l1_hbm, l2_hbm, out_ref,
                 v_ref, l1_ref, l2_ref, left, vs, cf, cf2, ce, hupraw, hloraw, rx, ry, wx, fy, wy, hup, hlo, chx, chy, ysend, yrecv,
                 own, xsend, xrecv, zsend, zrecv,
                 in_sem, hs_sem, hr_sem, xs_sem, xr_sem, zs_sem, zr_sem):
    gx = lax.axis_index("gx")
    gy = lax.axis_index("gy")
    ma = lax.axis_index("ma")
    other = 1 - gy
    rows = out_ref.shape[2]
    _, _, planes, sites, width = vs.shape
    zdim = ce.shape[1]
    f32 = jnp.float32
    tile = 16
    up, down = lax.rem(gx + 1, nx), lax.rem(gx + nx - 1, nx)

    staged = [
        pltpu.make_async_copy(src, dst, in_sem.at[i])
        for i, (src, dst) in enumerate(((v_hbm, v_ref), (l1_hbm, l1_ref), (l2_hbm, l2_ref)))
    ]
    barrier = pltpu.get_barrier_semaphore()
    for off in range(1, nx):
        pl.semaphore_signal(
            barrier, inc=1, device_id={"gx": lax.rem(gx + off, nx)}, device_id_type=MESH
        )
    for copy in staged:
        copy.start()
    pl.semaphore_signal(barrier, inc=1, device_id={"gy": other}, device_id_type=MESH)
    pl.semaphore_signal(barrier, inc=1, device_id={"ma": 1 - ma}, device_id_type=MESH)

    sel_row = lax.broadcasted_iota(jnp.int32, (sites, sites // zdim), 0)
    sel_col = lax.broadcasted_iota(jnp.int32, (sites, sites // zdim), 1)
    picks = [(sel_row == sel_col * zdim + z).astype(jnp.bfloat16) for z in range(zdim)]

    def relay(x, carry):
        for source, target in ((l1_ref, cf), (l2_ref, cf2)):
            raw = source[:, x].astype(f32)
            total = None
            for z in range(zdim):
                term = lax.dot_general(
                    picks[z], raw[:, z, :].astype(jnp.bfloat16),
                    (((1,), (1,)), ((), ())), preferred_element_type=f32,
                )
                total = term if total is None else total + term
            target[x] = total
            if source is l2_ref:
                ce[x] = total[sites - zdim :]
        for p in range(2):
            for c in range(3):
                vs[p, c, x] = v_ref[p, x, :, c].reshape(sites, width)
        return carry


    def send(i, src, dst, target):
        copy = pltpu.make_async_remote_copy(
            src_ref=src, dst_ref=dst, send_sem=hs_sem.at[i], recv_sem=hr_sem.at[i],
            device_id=target, device_id_type=MESH,
        )
        copy.start()
        return copy

    staged[0].wait()
    pl.semaphore_wait(barrier, nx + 1)
    copy_up = send(1, v_ref.at[:, planes - 1], hloraw, {"gx": up})
    copy_down = send(0, v_ref.at[:, 0], hupraw, {"gx": down})
    for copy in staged[1:]:
        copy.wait()
    lax.fori_loop(0, planes, relay, 0)
    copy_cx = send(2, cf.at[planes - 1], chx, {"gx": up})
    copy_cy = send(3, ce, chy, {"gy": other})
    span = planes * sites
    for p in range(2):
        for c in range(3):
            left[ma, p, :, c * span : (c + 1) * span] = vs[p, c].reshape(span, width).T
    copy_vt = send(4, left.at[ma], left.at[ma], {"ma": 1 - ma})

    def part(t):
        return pl.ds(t * tile, tile)

    def load(getter, t):
        real = [getter(0, c, t).astype(f32) for c in range(3)]
        imag = [getter(1, c, t).astype(f32) for c in range(3)]
        return real, imag

    def back_x(coefs, getter, slot, t):
        values = linked(coefs, *load(getter, t), True)
        for i in range(6):
            wx[slot, i, part(t)] = values[i]

    def fore_x(x, coefs, getter, edge_slot, t):
        values = linked(coefs, *load(getter, t), False)
        for i in range(6):
            value = (values[i] - wx[x, i, part(t)]).astype(rx.dtype)
            rx[i // 3, i % 3, x, part(t)] = value
            wide = value.astype(f32)
            if t == 0:
                ysend[0, edge_slot, i] = wide[:zdim].astype(ysend.dtype)
            if t == sites // tile - 1:
                ysend[1, edge_slot, i] = wide[tile - zdim :].astype(ysend.dtype)

    def plane(x):
        return lambda p, c, t: vs[p, c, x, part(t)]

    tiles = range(sites // tile)
    for t in tiles:
        back_x(cf[0, part(t)], plane(0), 1, t)

    def inner(x, carry):
        for t in tiles:
            coefs = cf[x, part(t)]
            back_x(coefs, plane(x), x + 1, t)
            fore_x(x, coefs, plane(x + 1), x - 1, t)
        return carry

    lax.fori_loop(1, planes - 1, inner, 0)
    inner_edges = planes - 2
    copies_y = [
        send(5 + s, ysend.at[s, pl.ds(0, inner_edges)], yrecv.at[s, pl.ds(0, inner_edges)],
             {"gy": other})
        for s in range(2)
    ]
    copy_cx.wait()
    copy_up.wait()
    for p in range(2):
        for c in range(3):
            hlo[p, c] = hloraw[p, :, c].reshape(sites, width)
    for t in tiles:
        back_x(chx[part(t)], lambda p, c, t: hlo[p, c, part(t)], 0, t)
        fore_x(0, cf[0, part(t)], plane(1), inner_edges, t)
    copy_down.wait()
    for p in range(2):
        for c in range(3):
            hup[p, c] = hupraw[p, :, c].reshape(sites, width)
    for t in tiles:
        fore_x(planes - 1, cf[planes - 1, part(t)],
               lambda p, c, t: hup[p, c, part(t)], inner_edges + 1, t)
    copies_y += [
        send(7 + s, ysend.at[s, pl.ds(inner_edges, 2)], yrecv.at[s, pl.ds(inner_edges, 2)],
             {"gy": other})
        for s in range(2)
    ]
    copy_vt.wait()

    offsets = sorted(range(1, nx), key=lambda o: -min(o, nx - o)) + [0]
    rights = (rx, ry)
    modes = left.shape[2]
    depth = left.shape[3]
    dot = functools.partial(jnp.dot, preferred_element_type=f32)
    x_copies, z_copies = {}, {}

    def project(k, d):
        c = 2 * k + d
        base = lax.rem(gx + offsets[k], nx) * (2 * rows)
        half = base // modes
        start = pl.multiple_of(base - half * modes, 2 * rows)
        left_real = left[half, 0, pl.ds(start, 2 * rows), :]
        left_imag = left[half, 1, pl.ds(start, 2 * rows), :]
        right_real = rights[d][0].reshape(depth, width)
        right_imag = rights[d][1].reshape(depth, width)
        real = dot(left_real, right_real) + dot(left_imag, right_imag)
        imag = dot(left_real, right_imag) - dot(left_imag, right_real)
        first = jnp.stack([real[:rows], imag[:rows]])
        second = jnp.stack([real[rows:], imag[rows:]])
        own[c] = jnp.where(gy == 0, first, second)
        xsend[c] = jnp.where(gy == 0, second, first).astype(xsend.dtype)
        copy = pltpu.make_async_remote_copy(
            src_ref=xsend.at[c], dst_ref=xrecv.at[c],
            send_sem=xs_sem.at[c], recv_sem=xr_sem.at[c],
            device_id={"gy": other}, device_id_type=MESH,
        )
        copy.start()
        x_copies[c] = copy

    def pass_on(k, d):
        c = 2 * k + d
        x_copies[c].wait()
        total = own[c] + xrecv[c].astype(f32)
        if offsets[k] == 0:
            own[c] = total
            return
        zsend[c] = total.astype(zsend.dtype)
        copy = pltpu.make_async_remote_copy(
            src_ref=zsend.at[c], dst_ref=zrecv.at[c],
            send_sem=zs_sem.at[c], recv_sem=zr_sem.at[c],
            device_id={"gx": lax.rem(gx + offsets[k], nx)}, device_id_type=MESH,
        )
        copy.start()
        z_copies[c] = copy

    for k in range(nx):
        project(k, 0)

    copy_cy.wait()
    for copy in copies_y:
        copy.wait()
    pad = 8

    def y_plane(x, slot):
        for i in range(6):
            fy[i, pad : pad + sites] = rx[i // 3, i % 3, x].astype(f32)
            fy[i, pad + sites : pad + sites + zdim] = yrecv[0, slot, i].astype(f32)
        low = [yrecv[1, slot, i].astype(f32) for i in range(6)]
        values = linked(chy[x], low[:3], low[3:], True)
        for i in range(6):
            wy[i, pad - zdim : pad] = values[i]
        for t in tiles:
            coefs = cf2[x, part(t)]
            here = [fy[i, pad + t * tile : pad + (t + 1) * tile] for i in range(6)]
            values = linked(coefs, here[:3], here[3:], True)
            for i in range(6):
                wy[i, pad + t * tile : pad + (t + 1) * tile] = values[i]
            ahead = [fy[i, pad + zdim + t * tile : pad + zdim + (t + 1) * tile] for i in range(6)]
            values = linked(coefs, ahead[:3], ahead[3:], False)
            for i in range(6):
                behind = wy[i, pad - zdim + t * tile : pad - zdim + (t + 1) * tile]
                ry[i // 3, i % 3, x, part(t)] = (values[i] - behind).astype(ry.dtype)

    def y_loop(x, carry):
        y_plane(x, jnp.where(x == 0, inner_edges, jnp.where(x == planes - 1, inner_edges + 1, x - 1)))
        return carry

    lax.fori_loop(0, planes, y_loop, 0)

    for k in range(nx):
        project(k, 1)
        pass_on(k, 0)
    for k in range(nx):
        pass_on(k, 1)
    last = 2 * (nx - 1)
    for d in range(2):
        total = own[last + d]
        for k in range(nx - 1):
            z_copies[2 * k + d].wait()
            total = total + zrecv[2 * k + d].astype(f32)
        out_ref[d] = total


def fused(eigen_modes, links_first, links_second):
    nx = lax.axis_size("gx")
    ny = lax.axis_size("gy")
    nm = lax.axis_size("ma")
    _, planes, ysize, zdim, _, width = eigen_modes.shape
    sites = ysize * zdim
    depth = 3 * planes * sites
    v = jnp.transpose(eigen_modes, (0, 1, 2, 4, 3, 5))

    def raw(links):
        return jnp.transpose(links, (0, 1, 2, 3, 5, 4)).reshape(18, planes, zdim, ysize)

    rows = width * nm // (nx * ny)
    count = 2 * nx
    bf16, f32 = jnp.bfloat16, jnp.float32
    vmem = pl.BlockSpec(memory_space=pltpu.VMEM)
    chunk = (2, rows, width)
    return pl.pallas_call(
        functools.partial(fused_kernel, nx),
        out_shape=jax.ShapeDtypeStruct((2, 2, rows, width), f32),
        in_specs=[pl.BlockSpec(memory_space=pltpu.HBM)] * 3,
        out_specs=vmem,
        scratch_shapes=[
            pltpu.VMEM((2, planes, ysize, 3, zdim, width), bf16),
            pltpu.VMEM((18, planes, zdim, ysize), bf16),
            pltpu.VMEM((18, planes, zdim, ysize), bf16),
            pltpu.VMEM((nm, 2, width, depth), bf16),
            pltpu.VMEM((2, 3, planes, sites, width), bf16),
            pltpu.VMEM((planes, sites, 18), f32),
            pltpu.VMEM((planes, sites, 18), f32),
            pltpu.VMEM((planes, zdim, 18), f32),
            pltpu.VMEM((2, ysize, 3, zdim, width), bf16),
            pltpu.VMEM((2, ysize, 3, zdim, width), bf16),
            pltpu.VMEM((2, 3, planes, sites, width), bf16),
            pltpu.VMEM((2, 3, planes, sites, width), bf16),
            pltpu.VMEM((planes, 6, sites, width), f32),
            pltpu.VMEM((6, sites + 16, width), f32),
            pltpu.VMEM((6, sites + 16, width), f32),
            pltpu.VMEM((2, 3, sites, width), bf16),
            pltpu.VMEM((2, 3, sites, width), bf16),
            pltpu.VMEM((sites, 18), f32),
            pltpu.VMEM((planes, zdim, 18), f32),
            pltpu.VMEM((2, planes, 6, zdim, width), bf16),
            pltpu.VMEM((2, planes, 6, zdim, width), bf16),
            pltpu.VMEM((count,) + chunk, f32),
            pltpu.VMEM((count,) + chunk, bf16),
            pltpu.VMEM((count,) + chunk, bf16),
            pltpu.VMEM((count - 2,) + chunk, bf16),
            pltpu.VMEM((count - 2,) + chunk, bf16),
            pltpu.SemaphoreType.DMA((3,)),
            pltpu.SemaphoreType.DMA((9,)),
            pltpu.SemaphoreType.DMA((9,)),
            pltpu.SemaphoreType.DMA((count,)),
            pltpu.SemaphoreType.DMA((count,)),
            pltpu.SemaphoreType.DMA((count - 2,)),
            pltpu.SemaphoreType.DMA((count - 2,)),
        ],
        compiler_params=pltpu.CompilerParams(
            collective_id=0, has_side_effects=True, vmem_limit_bytes=24 * 1024 * 1024
        ),
    )(*[pltpu.with_memory_space_constraint(a, pltpu.HBM) for a in (v, raw(links_first), raw(links_second))])


def local(eigen_modes, links_first, links_second):
    width = eigen_modes.shape[5]
    ng, ny, nm = lax.axis_size("gx"), lax.axis_size("gy"), lax.axis_size("ma")
    sites = eigen_modes.shape[2] * eigen_modes.shape[3]
    rows = width * nm // (ng * ny)
    aligned = rows % 16 == 0 and width % (2 * rows) == 0 and sites % 16 == 0
    if ny == 2 and nm == 2 and ng > 1 and aligned and eigen_modes.shape[1] > 2:
        return fused(eigen_modes, links_first, links_second)
    modes = jnp.transpose(eigen_modes, (0, 4, 1, 2, 3, 5))
    upper = shifted(modes[:, :, :1], "gx", -1)
    lower = shifted(modes[:, :, -1:], "gx", 1)
    lower_links = shifted(links_first[:, :, :, -1:], "gx", 1)
    lower_links_y = shifted(links_second[:, :, :, :, -1:], "gy", 1)
    field = modes.astype(jnp.float32)
    forward = jnp.concatenate([modes[:, :, 1:], upper], axis=2).astype(jnp.float32)
    linked = apply_link(links_first[:, :, :, :-1], field[:, :, :-1], True)
    behind = apply_link(lower_links, lower.astype(jnp.float32), True)
    backward = jnp.concatenate([behind, linked], axis=2)
    disp_x = (apply_link(links_first, forward, False) - backward).astype(jnp.bfloat16)
    upper_row = shifted(disp_x[:, :, :, :1], "gy", -1)
    lower_row = shifted(disp_x[:, :, :, -1:], "gy", 1)
    forward_y = jnp.concatenate([disp_x[:, :, :, 1:], upper_row], axis=3).astype(jnp.float32)
    linked_y = apply_link(links_second[:, :, :, :, :-1], disp_x[:, :, :, :-1].astype(jnp.float32), True)
    behind_y = apply_link(lower_links_y, lower_row.astype(jnp.float32), True)
    backward_y = jnp.concatenate([behind_y, linked_y], axis=3)
    disp_xy = (apply_link(links_second, forward_y, False) - backward_y).astype(jnp.bfloat16)
    right_x = disp_x.reshape(2, -1, width)
    right_y = disp_xy.reshape(2, -1, width)
    left = lax.all_gather(modes.reshape(2, -1, width), "ma", axis=2, tiled=True)
    outputs = []
    for right in (right_x, right_y):
        real_out = contract(left[0], right[0]) + contract(left[1], right[1])
        imag_out = contract(left[0], right[1]) - contract(left[1], right[0])
        outputs.append(jnp.stack([real_out, imag_out]))
    partial_terms = jnp.stack(outputs)
    across_x = lax.psum_scatter(partial_terms, "gx", scatter_dimension=2, tiled=True)
    return lax.psum_scatter(across_x, "gy", scatter_dimension=2, tiled=True)


def solution(mesh):
    return jax.shard_map(
        local,
        mesh=mesh,
        in_specs=(
            P("cuts", "gx", "gy", None, None, "ma"),
            P("cuts", None, None, "gx", "gy", None),
            P("cuts", None, None, "gx", "gy", None),
        ),
        out_specs=P("cuts", None, ("gx", "gy"), "ma"),
        check_vma=False,
    )
```
